1024 devices in a mesh: sub: 128 (over z_hi, y, x), slab: 8 (over z_lo, core).
Axes of the slice: x: 4, y: 8, z: 16 (z_hi: 4, z_lo: 4; z = z_hi * 4 + z_lo), core: 2. Of those that a mesh axis runs over, the one named last changes fastest.
Arguments:
- coarse_basis: bfloat16 [512, 64, 4000], P('sub', 'slab'), may hold values from -6 to 6
- jacobians: bfloat16 [4, 750, 750], replicated, may hold values from -0.21875 to 0.21875
- element_faces: int32 [20480, 6], P(('sub', 'slab')), may hold values from 1 to 58, as said below
- element_type: int32 [20480], P(('sub', 'slab')), may hold values from 0 to 3
- element_count: int32 [1024], P(('sub', 'slab')), may hold values from 1 to 20, 15360 in all
- vertex_ids: int32 [1024, 32], P(('sub', 'slab')), may hold values from 0 to 511, as said below
Outputs:
- second_image: bfloat16 [512, 64, 4000], P('sub', 'slab')
- coarse_matrix: float32 [512, 512], P('sub')
The draws below stay inside these ranges and needn't reach their ends.
Inputs may be any that keep to these rules, and one draw needn't show every extreme that they name: `element_faces`: each row names six different cells of the subdomain's extended face grid of (6) x (10) cells, numbered row-major, the own face blocks at rows 1 to 4 and columns 1 to 8; never one of the four corner cells. Each subdomain's live slots are its first element_count slots. `vertex_ids`: the 32 ids of one subdomain are different.
All inputs are finite; a program needn't handle non-finite values. No bound on the sum of `element_count` on one device may be relied on, other than what follows from the above.
Results may differ from the reference program's by a relative error of at most 0.0049.
Values may be sent and summed in bfloat16 or wider, within the bound.
No kernel may reach another device: no remote copies, remote signals or barrier semaphores. Data moves between devices by JAX's collectives and lax.ppermute only.
A program may use at most 64 MiB of HBM per device.

```python
import math
import jax
import jax.numpy as jnp
import numpy as np
from jax import lax

FD = 125
C = 32
ED = 750
JT = 4
FX = 4
FY = 8
E_CAP = 20
SUBDOMAINS = 1024
ELEMENTS = 20480
NV = 512
NX = 512
NY = 64
N_SUB = 128
N_SLAB = 8


def draw_element_faces(key, part):
    cells = (FX + 2) * (FY + 2)
    cell = jnp.arange(cells, dtype=jnp.int32)
    grid_row = cell // (FY + 2)
    grid_col = cell % (FY + 2)
    corner = ((grid_row == 0) | (grid_row == FX + 1)) & ((grid_col == 0) | (grid_col == FY + 1))
    scores = jax.random.randint(key, (ELEMENTS, cells), 0, 1 << 20, dtype=jnp.int32) * cells + cell[None, :]
    scores = jnp.where(corner[None, :], -1, scores)
    unused, picked = lax.top_k(scores, 6)
    return picked.astype(jnp.int32)


def draw_vertex_ids(key, part):
    vertex = jnp.arange(NV, dtype=jnp.int32)
    scores = jax.random.randint(key, (SUBDOMAINS, NV), 0, 1 << 16, dtype=jnp.int32) * NV + vertex[None, :]
    unused, picked = lax.top_k(scores, C)
    return picked.astype(jnp.int32)


def set_ends(values, rng, low, top_value):
    place = [jax.random.randint(jax.random.fold_in(rng, axis), (), 0, length) for axis, length in enumerate(values.shape)]
    main_axis = values.shape.index(max(values.shape))
    neighbour = place[:main_axis] + [(place[main_axis] + 1) % values.shape[main_axis]] + place[main_axis + 1:]
    return values.at[tuple(place)].set(low).at[tuple(neighbour)].set(top_value)


def shard_levels(stream_key, shape, cuts, smallest, top_value):
    def one(axis_at, shards_of):
        draws = jax.random.uniform(jax.random.fold_in(jax.random.fold_in(stream_key, 6), axis_at), (shards_of,), jnp.float32, smallest / len(cuts), top_value / len(cuts))
        return jnp.repeat(jnp.exp(draws), shape[axis_at] // shards_of).reshape((-1,) + (1,) * (len(shape) - axis_at - 1))

    loudness = one(*cuts[0])
    for cut in cuts[1:]:
        loudness = loudness * one(*cut)
    return loudness


def split_up(count, total, most, lean):
    loads = [(1 << 20) // math.isqrt(grade ** lean) + 1 for grade in range(2, count + 1)]
    surplus, holding = total - most - (count - 1), [1] * (count - 1)
    while surplus > 0:
        candidates = [i for i in range(count - 1) if holding[i] < most]
        whole, remaining = sum([loads[i] for i in candidates]), surplus
        for i in candidates:
            addition = min(most - holding[i], max(1, remaining * loads[i] // whole), surplus)
            holding[i] = holding[i] + addition
            surplus = surplus - addition
    return np.array([most] + holding)


def uneven(key, number_of, total, most, slope):
    if number_of == 2:
        one = jax.random.randint(key, (), max(1, total - most), min(most, total - 1) + 1)
        return jnp.stack([one, total - one])
    tallies = jnp.asarray(split_up(number_of, total, most, slope), jnp.int32)
    couples = (number_of - 1) // 2
    donor, sink = tallies[1:1 + 2 * couples:2], tallies[2:2 + 2 * couples:2]
    slack = jnp.minimum(donor - 1, most - sink)
    passed = jax.random.randint(jax.random.fold_in(key, 1), (couples,), 0, 1 << 20) % (slack + 1)
    tallies = tallies.at[1:1 + 2 * couples:2].set(donor - passed).at[2:2 + 2 * couples:2].set(sink + passed)
    return tallies[jax.random.permutation(jax.random.fold_in(key, 2), number_of)]


def centred(own_key, shape, width, limit, shards=(), kind=jnp.bfloat16):
    values = width * jax.random.normal(own_key, shape, jnp.float32)
    if shards:
        values = values * shard_levels(own_key, shape, shards, -0.22, 0.18)
    return jnp.clip(values, -limit, limit).astype(kind)


def setup_inputs(seed: int = 0) -> dict:
    keys = jax.random.split(jax.random.key(seed), 7)
    coarse_basis = centred(keys[0], (NX, NY, FD * C), 1.0, 6.0, ((0, 128), (1, 8)))
    jacobians = centred(keys[1], (JT, ED, ED), ED ** -0.5, 0.21875)
    element_faces = draw_element_faces(jax.random.fold_in(keys[6], 71), 0)
    element_type = set_ends(jax.random.randint(keys[3], (ELEMENTS,), 0, JT), jax.random.fold_in(keys[3], 1), 0, JT - 1).astype(jnp.int32)
    element_count = uneven(keys[4], SUBDOMAINS, SUBDOMAINS * E_CAP * 3 // 4, E_CAP, 1).astype(jnp.int32)
    vertex_ids = draw_vertex_ids(jax.random.fold_in(keys[6], 71), 0)
    return {"coarse_basis": coarse_basis, "jacobians": jacobians, "element_faces": element_faces, "element_type": element_type, "element_count": element_count, "vertex_ids": vertex_ids}


def apply_field(field, element_faces, element_type, element_count, jacobians):
    padded = jnp.pad(field, ((1, 1), (1, 1), (0, 0)))
    totals = jnp.zeros(padded.shape, jnp.float32)
    cells = (FX + 2) * (FY + 2)

    def one_domain(domain, totals):
        domain = jnp.asarray(domain).astype(jnp.int32)
        wide = (domain // N_SLAB).astype(jnp.int32)
        narrow = (domain % N_SLAB).astype(jnp.int32)
        zero = jnp.int32(0)
        start_x = (wide * FX).astype(jnp.int32)
        start_y = (narrow * FY).astype(jnp.int32)
        window = lax.dynamic_slice(padded, (start_x, start_y, zero), (FX + 2, FY + 2, FD * C)).reshape(cells, FD, C)
        first_slot = (domain * E_CAP).astype(jnp.int32)
        faces = lax.dynamic_slice_in_dim(element_faces, first_slot, E_CAP, 0)
        kinds = lax.dynamic_slice_in_dim(element_type, first_slot, E_CAP, 0)
        blocks = window[faces].reshape(E_CAP, 6 * FD, C).astype(jnp.float32)
        matrices = jacobians[kinds].astype(jnp.float32)
        product = jnp.einsum('ekl,elc->ekc', matrices, blocks)
        live = (jnp.arange(E_CAP, dtype=jnp.int32) < element_count[domain]).astype(jnp.float32)
        product = (product * live[:, None, None]).reshape(E_CAP * 6, FD, C)
        local = jnp.zeros((cells, FD, C), jnp.float32).at[faces.reshape(-1)].add(product)
        before = lax.dynamic_slice(totals, (start_x, start_y, zero), (FX + 2, FY + 2, FD * C))
        return lax.dynamic_update_slice(totals, before + local.reshape(FX + 2, FY + 2, FD * C), (start_x, start_y, zero))
    totals = lax.fori_loop(0, N_SUB * N_SLAB, one_domain, totals)
    return totals[1:-1, 1:-1]

def reference(coarse_basis, jacobians, element_faces, element_type, element_count, vertex_ids):
    first_image = apply_field(coarse_basis, element_faces, element_type, element_count, jacobians).astype(jnp.bfloat16)
    second_image = apply_field(first_image, element_faces, element_type, element_count, jacobians).astype(jnp.bfloat16)
    left = coarse_basis.reshape(N_SUB, FX, N_SLAB, FY, FD, C).astype(jnp.float32)
    right = first_image.reshape(N_SUB, FX, N_SLAB, FY, FD, C).astype(jnp.float32)
    local_coarse = jnp.einsum('afbgkc,afbgkd->abcd', left, right) * (1.0 / math.sqrt(FX * FY * FD))
    local_coarse = local_coarse.reshape(N_SUB * N_SLAB, C, C)
    coarse_matrix = jnp.zeros((NV, NV), jnp.float32).at[vertex_ids[:, :, None], vertex_ids[:, None, :]].add(local_coarse)
    return (second_image, coarse_matrix)
```

```python
import functools
import math

import jax
import jax.numpy as jnp
from jax import lax
from jax.experimental import pallas as pl
from jax.experimental.pallas import tpu as pltpu
from jax.sharding import PartitionSpec as P

FR = 32
LANES = 128
PACK = 4
VMEM_LIMIT = 50 * 1024 * 1024


def swap_slots(values):
    slot = lax.broadcasted_iota(jnp.int32, values[0].shape, 1) // 32
    upper = slot >= 2
    odd = slot % 2 == 1
    a, b, c, d = values
    a, c = jnp.where(upper, pltpu.roll(c, 64, 1), a), jnp.where(upper, c, pltpu.roll(a, 64, 1))
    b, d = jnp.where(upper, pltpu.roll(d, 64, 1), b), jnp.where(upper, d, pltpu.roll(b, 64, 1))
    a, b = jnp.where(odd, pltpu.roll(b, 32, 1), a), jnp.where(odd, b, pltpu.roll(a, 96, 1))
    c, d = jnp.where(odd, pltpu.roll(d, 32, 1), c), jnp.where(odd, d, pltpu.roll(c, 96, 1))
    return [a, b, c, d]


def plan_kernel(slots, faces_ref, type_ref, count_ref, cells_ref, kind_ref, total_ref):
    groups = kind_ref.shape[0]
    for i in range(groups * PACK * 6):
        cells_ref[i] = 0
    for i in range(groups):
        kind_ref[i] = 0
    count = count_ref[0]
    kinds = 4

    def tally(slot, sizes):
        live = slot < count
        return tuple(
            size + (live & (type_ref[slot] == kind)).astype(jnp.int32)
            for kind, size in enumerate(sizes)
        )

    sizes = lax.fori_loop(0, slots, tally, (jnp.int32(0),) * kinds)
    firsts, place = [], jnp.int32(0)
    for size in sizes:
        firsts.append(place)
        place = place + (size + PACK - 1) // PACK * PACK
    total_ref[0] = place // PACK

    def put(slot, nexts):
        kind = type_ref[slot]
        position = nexts[kinds - 1]
        for other in range(kinds - 1):
            position = jnp.where(kind == other, nexts[other], position)
        kind_ref[position // PACK] = kind
        for f in range(6):
            cells_ref[position * 6 + f] = faces_ref[slot, f]
        return tuple(at + (kind == other).astype(jnp.int32) for other, at in enumerate(nexts))

    lax.fori_loop(0, count, put, tuple(firsts))


def apply_kernel(
    flat, dims, cells_ref, kind_ref, total_ref, own_ref, up_ref, down_ref, left_ref, right_ref,
    jac_hbm, *rest
):
    rows, cols, dofs = dims
    edge = 6 * dofs
    width = cols + 2
    if flat:
        (t_ref, v_ref, to_up, to_down, to_left, to_right, field, totals, x_ref, y_ref, jac, sem) = rest
    else:
        (t_ref, to_up, to_down, to_left, to_right, field, totals, x_ref, y_ref, jac, sem) = rest

    fetch = pltpu.make_async_copy(jac_hbm, jac, sem)
    fetch.start()

    def cell_rows(cell):
        return pl.ds(pl.multiple_of(cell * FR, FR), FR)

    zero = jnp.zeros((FR, LANES), jnp.float32)
    field[0:FR, :] = zero
    if flat:
        sources = [(own_ref.at[r], (r + 1) * width + 1, 1, cols) for r in range(rows)]
        sources += [(up_ref, 1, 1, cols), (down_ref, (rows + 1) * width + 1, 1, cols)]
        sources += [(left_ref, width, width, rows), (right_ref, 2 * width - 1, width, rows)]
        for ref, first, step, many in sources:
            length = ref.shape[1]
            for a in range(FR):
                high = min(LANES * (a + 1), length)
                tile = ref[:, LANES * a : high].astype(jnp.float32)
                if high < LANES * (a + 1):
                    gap = jnp.zeros((many, LANES * (a + 1) - high), jnp.float32)
                    tile = jnp.concatenate([tile, gap], axis=1)
                field[pl.ds(first * FR + a, many, stride=step * FR), :] = tile
        for r in range(rows):
            for c in range(cols):
                cell = (r + 1) * width + c + 1
                v_ref[r * cols + c] = field[cell * FR : (cell + 1) * FR, :].astype(jnp.bfloat16)
    else:
        for r in range(rows):
            for c in range(cols):
                cell = (r + 1) * width + c + 1
                field[cell * FR : (cell + 1) * FR, :] = own_ref[r * cols + c].astype(jnp.float32)
        for c in range(cols):
            for ref, r in ((up_ref, 0), (down_ref, rows + 1)):
                cell = r * width + c + 1
                field[cell * FR : (cell + 1) * FR, :] = ref[c].astype(jnp.float32)
        for r in range(rows):
            for ref, c in ((left_ref, 0), (right_ref, cols + 1)):
                cell = (r + 1) * width + c
                field[cell * FR : (cell + 1) * FR, :] = ref[r].astype(jnp.float32)
    for cell in range((rows + 2) * width):
        totals[cell * FR : (cell + 1) * FR, :] = zero
    y_ref[edge // 8 * 8 :, :] = jnp.zeros((y_ref.shape[0] - edge // 8 * 8, LANES), jnp.float32)

    fetch.wait()

    def group(g, carry):
        kind = kind_ref[g]
        cells = [[cells_ref[(g * PACK + s) * 6 + f] for s in range(PACK)] for f in range(6)]
        for f in range(6):
            spread = swap_slots([field[cell_rows(cells[f][s]), :] for s in range(PACK)])
            for b in range(4):
                x_ref[pl.ds(f * dofs + b, FR, stride=4), :] = spread[b]
        y_ref[0:edge, :] = jnp.dot(
            jac[kind], x_ref[0:edge, :].astype(jnp.bfloat16), preferred_element_type=jnp.float32
        )
        for f in range(6):
            back = swap_slots([y_ref[pl.ds(f * dofs + b, FR, stride=4), :] for b in range(4)])
            for s in range(PACK):
                at = cell_rows(cells[f][s])
                totals[at, :] = totals[at, :] + back[s]
        return carry

    lax.fori_loop(0, total_ref[0], group, jnp.int32(0))

    for r in range(rows):
        for c in range(cols):
            cell = (r + 1) * width + c + 1
            t_ref[r * cols + c] = totals[cell * FR : (cell + 1) * FR, :]
    for c in range(cols):
        for ref, r in ((to_up, 0), (to_down, rows + 1)):
            cell = r * width + c + 1
            ref[c] = totals[cell * FR : (cell + 1) * FR, :].astype(jnp.bfloat16)
    for r in range(rows):
        for ref, c in ((to_left, 0), (to_right, cols + 1)):
            cell = (r + 1) * width + c
            ref[r] = totals[cell * FR : (cell + 1) * FR, :].astype(jnp.bfloat16)


def combined(dims, r, c, t_ref, up_ref, down_ref, left_ref, right_ref):
    rows, cols, dofs = dims
    value = t_ref[r * cols + c]
    if r == 0:
        value = value + up_ref[c].astype(jnp.float32)
    if r == rows - 1:
        value = value + down_ref[c].astype(jnp.float32)
    if c == 0:
        value = value + left_ref[r].astype(jnp.float32)
    if c == cols - 1:
        value = value + right_ref[r].astype(jnp.float32)
    return value


def middle_kernel(
    dims, t_ref, up_ref, down_ref, left_ref, right_ref, v_ref, ids_ref,
    w_ref, to_up, to_down, to_left, to_right, mail_ref
):
    rows, cols, dofs = dims
    row = lax.broadcasted_iota(jnp.int32, (FR, LANES), 0)
    slot = lax.broadcasted_iota(jnp.int32, (FR, LANES), 1) // 32
    real = row * 4 + slot < dofs
    for r in range(rows):
        for c in range(cols):
            value = combined(dims, r, c, t_ref, up_ref, down_ref, left_ref, right_ref)
            value = jnp.where(real, value, 0.0).astype(jnp.bfloat16)
            w_ref[r * cols + c] = value
            if r == 0:
                to_up[c] = value
            if r == rows - 1:
                to_down[c] = value
            if c == 0:
                to_left[r] = value
            if c == cols - 1:
                to_right[r] = value
    v = v_ref[...].reshape(rows * cols * FR, LANES)
    w = w_ref[...].reshape(rows * cols * FR, LANES)
    square = lax.dot_general(v, w, (((0,), (0,)), ((), ())), preferred_element_type=jnp.float32)
    side = lax.broadcasted_iota(jnp.int32, (LANES, LANES), 1) // 32
    diagonal = lax.broadcasted_iota(jnp.int32, (LANES, LANES), 0) // 32 == side
    square = jnp.where(diagonal, square, 0.0)
    local = square[0:32] + square[32:64] + square[64:96] + square[96:128]
    local = local + pltpu.roll(local, 64, 1)
    local = (local + pltpu.roll(local, 32, 1)) * (1.0 / math.sqrt(rows * cols * dofs))
    local = jnp.where(diagonal, jnp.concatenate([local] * 4, axis=0), 0.0)
    owners = mail_ref.shape[0]
    ids = ids_ref[...]
    owner = lax.broadcasted_iota(jnp.int32, (owners, LANES), 0)
    vertex = 4 * owner + lax.broadcasted_iota(jnp.int32, (owners, LANES), 1) // 32
    place = (vertex == ids).astype(jnp.bfloat16)
    high = local.astype(jnp.bfloat16)
    low = (local - high.astype(jnp.float32)).astype(jnp.bfloat16)
    mail_ref[:, 0, :] = jnp.dot(place, high, preferred_element_type=jnp.float32) + jnp.dot(
        place, low, preferred_element_type=jnp.float32
    )
    mail_ref[:, 1, :] = jnp.broadcast_to(ids.astype(jnp.float32), (owners, LANES))


def expand_kernel(mail_ref, out_ref, turned_ref, flat_ref, hot_ref):
    senders = mail_ref.shape[0]
    vertices = out_ref.shape[2]
    ids = mail_ref[:, 1, :]
    vertex = lax.broadcasted_iota(jnp.int32, (senders, vertices), 1).astype(jnp.float32)
    turned_ref[...] = mail_ref[:, 0, :].T
    for s in range(32):
        part = slice(s * senders, (s + 1) * senders)
        flat_ref[:, part] = turned_ref[pl.ds(s, 4, stride=32), :]
        hot_ref[part, :] = (ids[:, s : s + 1] == vertex).astype(jnp.bfloat16)
    values = flat_ref[...]
    high = values.astype(jnp.bfloat16).astype(jnp.float32)
    both = jnp.concatenate([high, values - high], axis=0).astype(jnp.bfloat16)
    wide = jnp.dot(both, hot_ref[...], preferred_element_type=jnp.float32)
    total = wide[0:4] + wide[4:8]
    for j in range(out_ref.shape[0]):
        out_ref[j] = total


def last_kernel(dims, t_ref, up_ref, down_ref, left_ref, right_ref, out_ref, hold):
    rows, cols, dofs = dims
    length = out_ref.shape[2]
    for r in range(rows):
        for c in range(cols):
            value = combined(dims, r, c, t_ref, up_ref, down_ref, left_ref, right_ref)
            hold[pl.ds(r * FR * cols + c, FR, stride=cols), :] = value
    for r in range(rows):
        for a in range(FR):
            high = min(LANES * (a + 1), length)
            start = (r * FR + a) * cols
            tile = hold[start : start + cols, 0 : high - LANES * a]
            out_ref[r, :, LANES * a : high] = tile.astype(jnp.bfloat16)


VM = pl.BlockSpec(memory_space=pltpu.VMEM)
SM = pl.BlockSpec(memory_space=pltpu.SMEM)
HBM = pl.BlockSpec(memory_space=pltpu.HBM)


def struct(shape, dtype=jnp.bfloat16):
    return jax.ShapeDtypeStruct(shape, dtype)


def plan(element_faces, element_type, element_count):
    slots = element_faces.shape[0]
    groups = (slots + 3 * 4) // PACK + 1
    return pl.pallas_call(
        functools.partial(plan_kernel, slots),
        out_shape=(
            struct((groups * PACK * 6,), jnp.int32),
            struct((groups,), jnp.int32),
            struct((1,), jnp.int32),
        ),
        in_specs=[SM] * 3,
        out_specs=(SM,) * 3,
        name="plan",
    )(element_faces, element_type, element_count)


def rim_structs(rows, cols):
    return (
        struct((cols, FR, LANES)),
        struct((cols, FR, LANES)),
        struct((rows, FR, LANES)),
        struct((rows, FR, LANES)),
    )


def apply(flat, dims, table, own, rims, jacobians):
    rows, cols, dofs = dims
    cells = rows * cols
    out = (struct((cells, FR, LANES), jnp.float32),)
    if flat:
        out += (struct((cells, FR, LANES)),)
    out += rim_structs(rows, cols)
    area = (rows + 2) * (cols + 2) * FR
    flops = 2 * 16 * 36 * dofs * dofs * 32
    moved = jacobians.size * 2 + cells * FR * LANES * 6
    return pl.pallas_call(
        functools.partial(apply_kernel, flat, dims),
        out_shape=out,
        in_specs=[SM] * 3 + [VM] * 5 + [HBM],
        out_specs=(VM,) * len(out),
        scratch_shapes=[
            pltpu.VMEM((area, LANES), jnp.float32),
            pltpu.VMEM((area, LANES), jnp.float32),
            pltpu.VMEM((6 * dofs + 10, LANES), jnp.float32),
            pltpu.VMEM((6 * dofs + 10, LANES), jnp.float32),
            pltpu.VMEM(jacobians.shape, jnp.bfloat16),
            pltpu.SemaphoreType.DMA,
        ],
        compiler_params=pltpu.CompilerParams(vmem_limit_bytes=VMEM_LIMIT),
        cost_estimate=pl.CostEstimate(flops=flops, bytes_accessed=moved, transcendentals=0),
        name="apply_flat" if flat else "apply_tiles",
    )(*table, own, *rims, jacobians)


def middle(dims, total, rims, tiles, ids, owners):
    rows, cols, dofs = dims
    cells = rows * cols
    return pl.pallas_call(
        functools.partial(middle_kernel, dims),
        out_shape=(struct((cells, FR, LANES)),)
        + rim_structs(rows, cols)
        + (struct((owners, 2, LANES), jnp.float32),),
        in_specs=[VM] * 7,
        out_specs=(VM,) * 6,
        compiler_params=pltpu.CompilerParams(vmem_limit_bytes=VMEM_LIMIT),
        cost_estimate=pl.CostEstimate(flops=2**26, bytes_accessed=2**20, transcendentals=0),
        name="middle",
    )(total, *rims, tiles, ids)


def expand(mail, narrow, vertex_total):
    owned = vertex_total // mail.shape[0]
    return pl.pallas_call(
        expand_kernel,
        out_shape=struct((narrow, owned, vertex_total), jnp.float32),
        in_specs=[VM],
        out_specs=VM,
        scratch_shapes=[
            pltpu.VMEM((LANES, mail.shape[0]), jnp.float32),
            pltpu.VMEM((owned, 32 * mail.shape[0]), jnp.float32),
            pltpu.VMEM((32 * mail.shape[0], vertex_total), jnp.bfloat16),
        ],
        compiler_params=pltpu.CompilerParams(vmem_limit_bytes=VMEM_LIMIT),
        cost_estimate=pl.CostEstimate(flops=2**30, bytes_accessed=2**18, transcendentals=0),
        name="expand",
    )(mail)


def last(dims, total, rims, length):
    rows, cols, dofs = dims
    return pl.pallas_call(
        functools.partial(last_kernel, dims),
        out_shape=struct((rows, cols, length)),
        in_specs=[VM] * 5,
        out_specs=VM,
        scratch_shapes=[pltpu.VMEM((rows * cols * FR, LANES), jnp.float32)],
        compiler_params=pltpu.CompilerParams(vmem_limit_bytes=VMEM_LIMIT),
        name="last",
    )(total, *rims)


def exchange(to_up, to_down, to_left, to_right):
    def ring(axis):
        peers = lax.axis_size(axis)
        ahead = [(i, i + 1) for i in range(peers - 1)]
        return ahead, [(j, i) for i, j in ahead]

    ahead, back = ring("sub")
    from_up = lax.ppermute(to_down, "sub", ahead)
    from_down = lax.ppermute(to_up, "sub", back)
    ahead, back = ring("slab")
    from_left = lax.ppermute(to_right, "slab", ahead)
    from_right = lax.ppermute(to_left, "slab", back)
    return from_up, from_down, from_left, from_right


def body(coarse_basis, jacobians, element_faces, element_type, element_count, vertex_ids):
    rows, cols, length = coarse_basis.shape
    dofs = jacobians.shape[1] // 6
    dims = (rows, cols, dofs)
    owners, narrow = lax.axis_size("sub"), lax.axis_size("slab")
    ids = jnp.tile(vertex_ids, (1, 4))

    rims = exchange(coarse_basis[0], coarse_basis[rows - 1], coarse_basis[:, 0], coarse_basis[:, cols - 1])
    table = plan(element_faces, element_type, element_count)
    total, tiles, *sent = apply(True, dims, table, coarse_basis, rims, jacobians)
    first, *halo, mail = middle(dims, total, exchange(*sent), tiles, ids, owners)
    mail = lax.all_to_all(mail, "sub", 0, 0)
    rims = exchange(*halo)
    total, *sent = apply(False, dims, table, first, rims, jacobians)
    rims = exchange(*sent)
    mail, unused = lax.optimization_barrier((mail, rims[0]))
    parts = lax.all_to_all(expand(mail, narrow, rows * owners), "slab", 0, 0)
    second_image = last(dims, total, rims, length)
    return second_image, parts.sum(0)


def solution(mesh):
    return jax.shard_map(
        body,
        mesh=mesh,
        in_specs=(
            P("sub", "slab", None),
            P(),
            P(("sub", "slab"), None),
            P(("sub", "slab")),
            P(("sub", "slab")),
            P(("sub", "slab"), None),
        ),
        out_specs=(P("sub", "slab", None), P("sub", None)),
        check_vma=False,
    )
```

```python
import functools
import math

import jax
import jax.numpy as jnp
from jax import lax
from jax.experimental import pallas as pl
from jax.experimental.pallas import tpu as pltpu
from jax.sharding import PartitionSpec as P

FR = 32
LANES = 128
PACK = 4
VMEM_LIMIT = 50 * 1024 * 1024


def swap_slots(values):
    slot = lax.broadcasted_iota(jnp.int32, values[0].shape, 1) // 32
    upper = slot >= 2
    odd = slot % 2 == 1
    a, b, c, d = values
    a, c = jnp.where(upper, pltpu.roll(c, 64, 1), a), jnp.where(upper, c, pltpu.roll(a, 64, 1))
    b, d = jnp.where(upper, pltpu.roll(d, 64, 1), b), jnp.where(upper, d, pltpu.roll(b, 64, 1))
    a, b = jnp.where(odd, pltpu.roll(b, 32, 1), a), jnp.where(odd, b, pltpu.roll(a, 96, 1))
    c, d = jnp.where(odd, pltpu.roll(d, 32, 1), c), jnp.where(odd, d, pltpu.roll(c, 96, 1))
    return [a, b, c, d]


def make_plan(slots, groups, faces_ref, type_ref, count_ref, table_ref):
    kind_at = groups * PACK * 6
    for i in range(kind_at):
        table_ref[i] = 0
    count = count_ref[0]
    kinds = 4

    def tally(slot, sizes):
        live = slot < count
        return tuple(
            size + (live & (type_ref[slot] == kind)).astype(jnp.int32)
            for kind, size in enumerate(sizes)
        )

    sizes = lax.fori_loop(0, slots, tally, (jnp.int32(0),) * kinds)
    firsts, place = [], jnp.int32(0)
    for size in sizes:
        firsts.append(place)
        place = place + (size + PACK - 1) // PACK * PACK
    table_ref[kind_at + groups] = place // PACK

    def put(slot, nexts):
        kind = type_ref[slot]
        position = nexts[kinds - 1]
        for other in range(kinds - 1):
            position = jnp.where(kind == other, nexts[other], position)
        table_ref[kind_at + position // PACK] = kind
        for f in range(6):
            table_ref[position * 6 + f] = faces_ref[f, slot]
        return tuple(at + (kind == other).astype(jnp.int32) for other, at in enumerate(nexts))

    lax.fori_loop(0, count, put, tuple(firsts))


def sides(side_ref, rows, cols):
    odd_row, odd_col = side_ref[0] == 1, side_ref[1] == 1
    first_row = jnp.where(odd_row, 0, rows - 1)
    first_col = jnp.where(odd_col, 0, cols - 1)
    return (first_row, rows - 1 - first_row), (first_col, cols - 1 - first_col)


def beyond(edge, length):
    return jnp.where(edge == 0, 0, length + 1)


def apply_kernel(flat, dims, groups, *refs):
    rows, cols, dofs = dims
    edge = 6 * dofs
    width = cols + 2
    if flat:
        side_ref, faces_ref, type_ref, count_ref, own_ref, *refs = refs
    else:
        side_ref, table_ref, own_ref, *refs = refs
    row_refs, col_refs, jac_hbm, t_ref = refs[0:2], refs[2:4], refs[4], refs[5]
    to_rows, to_cols = refs[6:8], refs[8:10]
    if flat:
        v_ref, table_ref = refs[10:12]
    field, totals, x_ref, y_ref, jac, sem = refs[-6:]
    fetch = pltpu.make_async_copy(jac_hbm, jac, sem)
    fetch.start()
    if flat:
        make_plan(type_ref.shape[0], groups, faces_ref, type_ref, count_ref, table_ref)
    row_edges, col_edges = sides(side_ref, rows, cols)
    out_rows = [beyond(r, rows) for r in row_edges]
    out_cols = [beyond(c, cols) for c in col_edges]

    def cell_rows(cell):
        if isinstance(cell, int):
            return slice(cell * FR, (cell + 1) * FR)
        return pl.ds(pl.multiple_of(cell * FR, FR), FR)

    zero = jnp.zeros((FR, LANES), jnp.float32)
    field[0:FR, :] = zero
    if flat:
        sources = [(own_ref.at[r], (r + 1) * width + 1, 1, cols) for r in range(rows)]
        sources += [(row_refs[n], out_rows[n] * width + 1, 1, cols) for n in range(2)]
        sources += [(col_refs[n], width + out_cols[n], width, rows) for n in range(2)]
        for ref, first, step, many in sources:
            length = ref.shape[1]
            for a in range(FR):
                high = min(LANES * (a + 1), length)
                tile = ref[:, LANES * a : high].astype(jnp.float32)
                if high < LANES * (a + 1):
                    gap = jnp.zeros((many, LANES * (a + 1) - high), jnp.float32)
                    tile = jnp.concatenate([tile, gap], axis=1)
                field[pl.ds(first * FR + a, many, stride=step * FR), :] = tile
        for r in range(rows):
            for c in range(cols):
                v_ref[r * cols + c] = field[cell_rows((r + 1) * width + c + 1), :].astype(jnp.bfloat16)
    else:
        for r in range(rows):
            for c in range(cols):
                field[cell_rows((r + 1) * width + c + 1), :] = own_ref[r * cols + c].astype(jnp.float32)
        for n in range(2):
            for c in range(cols):
                field[cell_rows(out_rows[n] * width + c + 1), :] = row_refs[n][c].astype(jnp.float32)
            for r in range(rows):
                field[cell_rows((r + 1) * width + out_cols[n]), :] = col_refs[n][r].astype(jnp.float32)
    for cell in range((rows + 2) * width):
        totals[cell_rows(cell), :] = zero
    y_ref[edge // 8 * 8 :, :] = jnp.zeros((y_ref.shape[0] - edge // 8 * 8, LANES), jnp.float32)
    fetch.wait()

    def group(g, carry):
        kind = table_ref[groups * PACK * 6 + g]
        cells = [[table_ref[(g * PACK + s) * 6 + f] for s in range(PACK)] for f in range(6)]
        for f in range(6):
            spread = swap_slots([field[cell_rows(cells[f][s]), :] for s in range(PACK)])
            for b in range(4):
                x_ref[pl.ds(f * dofs + b, FR, stride=4), :] = spread[b]
        y_ref[0:edge, :] = jnp.dot(
            jac[kind], x_ref[0:edge, :].astype(jnp.bfloat16), preferred_element_type=jnp.float32
        )
        for f in range(6):
            back = swap_slots([y_ref[pl.ds(f * dofs + b, FR, stride=4), :] for b in range(4)])
            for s in range(PACK):
                at = cell_rows(cells[f][s])
                totals[at, :] = totals[at, :] + back[s]
        return carry

    lax.fori_loop(0, table_ref[groups * PACK * 6 + groups], group, jnp.int32(0))

    for r in range(rows):
        for c in range(cols):
            t_ref[r * cols + c] = totals[cell_rows((r + 1) * width + c + 1), :]
    for n in range(2):
        for c in range(cols):
            to_rows[n][c] = totals[cell_rows(out_rows[n] * width + c + 1), :].astype(jnp.bfloat16)
        for r in range(rows):
            to_cols[n][r] = totals[cell_rows((r + 1) * width + out_cols[n]), :].astype(jnp.bfloat16)


def combine(dims, side_ref, t_ref, rims, hold):
    rows, cols, dofs = dims
    row_edges, col_edges = sides(side_ref, rows, cols)
    for cell in range(rows * cols):
        hold[cell] = t_ref[cell]
    for n in range(2):
        for c in range(cols):
            cell = row_edges[n] * cols + c
            hold[cell] = hold[cell] + rims[n][c].astype(jnp.float32)
        for r in range(rows):
            cell = r * cols + col_edges[n]
            hold[cell] = hold[cell] + rims[2 + n][r].astype(jnp.float32)
    return row_edges, col_edges


def middle_kernel(dims, side_ref, t_ref, a_ref, b_ref, c_ref, d_ref, w_ref, *refs):
    rows, cols, dofs = dims
    hold = refs[-1]
    to_rows, to_cols = refs[0:2], refs[2:4]
    row_edges, col_edges = combine(dims, side_ref, t_ref, (a_ref, b_ref, c_ref, d_ref), hold)
    row = lax.broadcasted_iota(jnp.int32, (FR, LANES), 0)
    slot = lax.broadcasted_iota(jnp.int32, (FR, LANES), 1) // 32
    real = row * 4 + slot < dofs
    for cell in range(rows * cols):
        w_ref[cell] = jnp.where(real, hold[cell], 0.0).astype(jnp.bfloat16)
    for n in range(2):
        for c in range(cols):
            to_rows[n][c] = w_ref[row_edges[n] * cols + c]
        for r in range(rows):
            to_cols[n][r] = w_ref[r * cols + col_edges[n]]


def mail_kernel(dims, v_ref, w_ref, ids_ref, mail_ref):
    rows, cols, dofs = dims
    v = v_ref[...].reshape(rows * cols * FR, LANES)
    w = w_ref[...].reshape(rows * cols * FR, LANES)
    square = lax.dot_general(v, w, (((0,), (0,)), ((), ())), preferred_element_type=jnp.float32)
    side = lax.broadcasted_iota(jnp.int32, (LANES, LANES), 1) // 32
    diagonal = lax.broadcasted_iota(jnp.int32, (LANES, LANES), 0) // 32 == side
    square = jnp.where(diagonal, square, 0.0)
    local = square[0:32] + square[32:64] + square[64:96] + square[96:128]
    local = local + pltpu.roll(local, 64, 1)
    local = (local + pltpu.roll(local, 32, 1)) * (1.0 / math.sqrt(rows * cols * dofs))
    local = jnp.where(diagonal, jnp.concatenate([local] * 4, axis=0), 0.0)
    owners = mail_ref.shape[0]
    ids = ids_ref[...]
    owner = lax.broadcasted_iota(jnp.int32, (owners, LANES), 0)
    vertex = 4 * owner + lax.broadcasted_iota(jnp.int32, (owners, LANES), 1) // 32
    place = (vertex == ids).astype(jnp.bfloat16)
    high = local.astype(jnp.bfloat16)
    low = (local - high.astype(jnp.float32)).astype(jnp.bfloat16)
    mail_ref[:, 0, :] = jnp.dot(place, high, preferred_element_type=jnp.float32) + jnp.dot(
        place, low, preferred_element_type=jnp.float32
    )
    mail_ref[:, 1, :] = jnp.broadcast_to(ids.astype(jnp.float32), (owners, LANES))


def expand_kernel(mail_ref, out_ref, turned_ref, flat_ref, hot_ref):
    senders = mail_ref.shape[0]
    vertices = out_ref.shape[2]
    ids = mail_ref[:, 1, :]
    vertex = lax.broadcasted_iota(jnp.int32, (senders, vertices), 1).astype(jnp.float32)
    turned_ref[...] = mail_ref[:, 0, :].T
    for s in range(32):
        part = slice(s * senders, (s + 1) * senders)
        flat_ref[:, part] = turned_ref[pl.ds(s, 4, stride=32), :]
        hot_ref[part, :] = (ids[:, s : s + 1] == vertex).astype(jnp.bfloat16)
    values = flat_ref[...]
    high = values.astype(jnp.bfloat16).astype(jnp.float32)
    both = jnp.concatenate([high, values - high], axis=0).astype(jnp.bfloat16)
    wide = jnp.dot(both, hot_ref[...], preferred_element_type=jnp.float32)
    total = wide[0:4] + wide[4:8]
    for j in range(out_ref.shape[0]):
        out_ref[j] = total


def last_kernel(dims, side_ref, t_ref, a_ref, b_ref, c_ref, d_ref, out_ref, sums, hold):
    rows, cols, dofs = dims
    length = out_ref.shape[2]
    combine(dims, side_ref, t_ref, (a_ref, b_ref, c_ref, d_ref), sums)
    for r in range(rows):
        for c in range(cols):
            hold[pl.ds(r * FR * cols + c, FR, stride=cols), :] = sums[r * cols + c]
    for r in range(rows):
        for a in range(FR):
            high = min(LANES * (a + 1), length)
            start = (r * FR + a) * cols
            tile = hold[start : start + cols, 0 : high - LANES * a]
            out_ref[r, :, LANES * a : high] = tile.astype(jnp.bfloat16)


VM = pl.BlockSpec(memory_space=pltpu.VMEM)
SM = pl.BlockSpec(memory_space=pltpu.SMEM)
HBM = pl.BlockSpec(memory_space=pltpu.HBM)


def struct(shape, dtype=jnp.bfloat16):
    return jax.ShapeDtypeStruct(shape, dtype)


def rim_structs(rows, cols):
    return (
        struct((cols, FR, LANES)),
        struct((cols, FR, LANES)),
        struct((rows, FR, LANES)),
        struct((rows, FR, LANES)),
    )


def apply(flat, dims, side, scalars, own, rims, jacobians):
    rows, cols, dofs = dims
    cells = rows * cols
    slots = scalars[1].shape[0] if flat else 0
    groups = (slots + 3 * 4) // PACK if flat else (scalars[0].shape[0] - 1) // (PACK * 6 + 1)
    out = (struct((cells, FR, LANES), jnp.float32),) + rim_structs(rows, cols)
    places = (VM,) * 5
    if flat:
        out += (struct((cells, FR, LANES)), struct((groups * (PACK * 6 + 1) + 1,), jnp.int32))
        places += (VM, SM)
    area = (rows + 2) * (cols + 2) * FR
    flops = 2**34
    moved = jacobians.size * 2 + cells * FR * LANES * 6
    return pl.pallas_call(
        functools.partial(apply_kernel, flat, dims, groups),
        out_shape=out,
        in_specs=[SM] * (1 + len(scalars)) + [VM] * 5 + [HBM],
        out_specs=places,
        scratch_shapes=[
            pltpu.VMEM((area, LANES), jnp.float32),
            pltpu.VMEM((area, LANES), jnp.float32),
            pltpu.VMEM((6 * dofs + 10, LANES), jnp.float32),
            pltpu.VMEM((6 * dofs + 10, LANES), jnp.float32),
            pltpu.VMEM(jacobians.shape, jnp.bfloat16),
            pltpu.SemaphoreType.DMA,
        ],
        compiler_params=pltpu.CompilerParams(vmem_limit_bytes=VMEM_LIMIT),
        cost_estimate=pl.CostEstimate(flops=flops, bytes_accessed=moved, transcendentals=0),
        name="apply_flat" if flat else "apply_tiles",
    )(side, *scalars, own, *rims, jacobians)


def middle(dims, side, total, rims):
    rows, cols, dofs = dims
    cells = rows * cols
    return pl.pallas_call(
        functools.partial(middle_kernel, dims),
        out_shape=(struct((cells, FR, LANES)),) + rim_structs(rows, cols),
        in_specs=[SM] + [VM] * 5,
        out_specs=(VM,) * 5,
        scratch_shapes=[pltpu.VMEM((cells, FR, LANES), jnp.float32)],
        compiler_params=pltpu.CompilerParams(vmem_limit_bytes=VMEM_LIMIT),
        name="middle",
    )(side, total, *rims)


def make_mail(dims, tiles, first, ids, owners):
    return pl.pallas_call(
        functools.partial(mail_kernel, dims),
        out_shape=struct((owners, 2, LANES), jnp.float32),
        in_specs=[VM] * 3,
        out_specs=VM,
        compiler_params=pltpu.CompilerParams(vmem_limit_bytes=VMEM_LIMIT),
        cost_estimate=pl.CostEstimate(flops=2**30, bytes_accessed=2**20, transcendentals=0),
        name="mail",
    )(tiles, first, ids)


def expand(mail, narrow, vertex_total):
    owned = vertex_total // mail.shape[0]
    return pl.pallas_call(
        expand_kernel,
        out_shape=struct((narrow, owned, vertex_total), jnp.float32),
        in_specs=[VM],
        out_specs=VM,
        scratch_shapes=[
            pltpu.VMEM((LANES, mail.shape[0]), jnp.float32),
            pltpu.VMEM((owned, 32 * mail.shape[0]), jnp.float32),
            pltpu.VMEM((32 * mail.shape[0], vertex_total), jnp.bfloat16),
        ],
        compiler_params=pltpu.CompilerParams(vmem_limit_bytes=VMEM_LIMIT),
        cost_estimate=pl.CostEstimate(flops=2**30, bytes_accessed=2**18, transcendentals=0),
        name="expand",
    )(mail)


def last(dims, side, total, rims, length):
    rows, cols, dofs = dims
    cells = rows * cols
    return pl.pallas_call(
        functools.partial(last_kernel, dims),
        out_shape=struct((rows, cols, length)),
        in_specs=[SM] + [VM] * 5,
        out_specs=VM,
        scratch_shapes=[
            pltpu.VMEM((cells, FR, LANES), jnp.float32),
            pltpu.VMEM((cells * FR, LANES), jnp.float32),
        ],
        compiler_params=pltpu.CompilerParams(vmem_limit_bytes=VMEM_LIMIT),
        cost_estimate=pl.CostEstimate(flops=2**34, bytes_accessed=2**20, transcendentals=0),
        name="last",
    )(side, total, *rims)


def exchange(row_first, row_second, col_first, col_second):
    def swap(value, axis, start):
        peers = lax.axis_size(axis)
        pairs = [(i, i + 1) for i in range(start, peers - 1, 2)]
        return lax.ppermute(value, axis, pairs + [(j, i) for i, j in pairs])

    second = swap(row_second, "sub", 1)
    return (
        swap(row_first, "sub", 0),
        second,
        swap(col_first, "slab", 0),
        swap(col_second, "slab", 1),
    )


def body(coarse_basis, jacobians, element_faces, element_type, element_count, vertex_ids):
    rows, cols, length = coarse_basis.shape
    dofs = jacobians.shape[1] // 6
    dims = (rows, cols, dofs)
    owners, narrow = lax.axis_size("sub"), lax.axis_size("slab")
    ids = jnp.tile(vertex_ids, (1, 4))
    odd_row, odd_col = lax.axis_index("sub") & 1, lax.axis_index("slab") & 1
    side = jnp.stack([odd_row, odd_col])

    ends = coarse_basis[0], coarse_basis[rows - 1], coarse_basis[:, 0], coarse_basis[:, cols - 1]
    rims = exchange(
        jnp.where(odd_row == 1, ends[0], ends[1]),
        jnp.where(odd_row == 1, ends[1], ends[0]),
        jnp.where(odd_col == 1, ends[2], ends[3]),
        jnp.where(odd_col == 1, ends[3], ends[2]),
    )
    scalars = (element_faces.T, element_type, element_count)
    total, *sent, tiles, table = apply(True, dims, side, scalars, coarse_basis, rims, jacobians)
    first, *halo = middle(dims, side, total, exchange(*sent))
    rims = exchange(*halo)
    tiles, unused = lax.optimization_barrier((tiles, rims[2]))
    mail = lax.all_to_all(make_mail(dims, tiles, first, ids, owners), "sub", 0, 0)
    total, *sent = apply(False, dims, side, (table,), first, rims, jacobians)
    rims = exchange(*sent)
    mail, unused = lax.optimization_barrier((mail, rims[2]))
    parts = lax.all_to_all(expand(mail, narrow, rows * owners), "slab", 0, 0)
    second_image = last(dims, side, total, rims, length)
    return second_image, parts.sum(0)


def solution(mesh):
    return jax.shard_map(
        body,
        mesh=mesh,
        in_specs=(
            P("sub", "slab", None),
            P(),
            P(("sub", "slab"), None),
            P(("sub", "slab")),
            P(("sub", "slab")),
            P(("sub", "slab"), None),
        ),
        out_specs=(P("sub", "slab", None), P("sub", None)),
        check_vma=False,
    )
```

```python
import functools
import math

import jax
import jax.numpy as jnp
from jax import lax
from jax.experimental import pallas as pl
from jax.experimental.pallas import tpu as pltpu
from jax.sharding import PartitionSpec as P

FR = 32
LANES = 128
PACK = 4
VMEM_LIMIT = 50 * 1024 * 1024


def swap_slots(values):
    slot = lax.broadcasted_iota(jnp.int32, values[0].shape, 1) // 32
    upper = slot >= 2
    odd = slot % 2 == 1
    a, b, c, d = values
    a, c = jnp.where(upper, pltpu.roll(c, 64, 1), a), jnp.where(upper, c, pltpu.roll(a, 64, 1))
    b, d = jnp.where(upper, pltpu.roll(d, 64, 1), b), jnp.where(upper, d, pltpu.roll(b, 64, 1))
    a, b = jnp.where(odd, pltpu.roll(b, 32, 1), a), jnp.where(odd, b, pltpu.roll(a, 96, 1))
    c, d = jnp.where(odd, pltpu.roll(d, 32, 1), c), jnp.where(odd, d, pltpu.roll(c, 96, 1))
    return [a, b, c, d]


def make_plan(slots, groups, faces_ref, type_ref, count_ref, table_ref):
    kind_at = groups * PACK * 6
    for i in range(kind_at):
        table_ref[i] = 0
    count = count_ref[0]
    kinds = 4

    def tally(slot, sizes):
        live = slot < count
        return tuple(
            size + (live & (type_ref[slot] == kind)).astype(jnp.int32)
            for kind, size in enumerate(sizes)
        )

    sizes = lax.fori_loop(0, slots, tally, (jnp.int32(0),) * kinds)
    firsts, place = [], jnp.int32(0)
    for kind, size in enumerate(sizes):
        firsts.append(place)
        place = place + (size + PACK - 1) // PACK * PACK
        table_ref[kind_at + groups + kind] = place // PACK

    def put(slot, nexts):
        kind = type_ref[slot]
        position = nexts[kinds - 1]
        for other in range(kinds - 1):
            position = jnp.where(kind == other, nexts[other], position)
        table_ref[kind_at + position // PACK] = kind
        for f in range(6):
            table_ref[position * 6 + f] = faces_ref[f, slot]
        return tuple(at + (kind == other).astype(jnp.int32) for other, at in enumerate(nexts))

    lax.fori_loop(0, count, put, tuple(firsts))


def sides(side_ref, rows, cols):
    odd_row, odd_col = side_ref[0] == 1, side_ref[1] == 1
    first_row = jnp.where(odd_row, 0, rows - 1)
    first_col = jnp.where(odd_col, 0, cols - 1)
    return (rows - 1 - first_row, first_row), (first_col, cols - 1 - first_col)


def beyond(edge, length):
    return jnp.where(edge == 0, 0, length + 1)


def apply_kernel(flat, dims, groups, *refs):
    rows, cols, dofs = dims
    edge = 6 * dofs
    width = cols + 2
    if flat:
        side_ref, faces_ref, type_ref, count_ref, own_ref, *refs = refs
    else:
        side_ref, table_ref, own_ref, *refs = refs
    row_refs, col_refs, jac_hbm, t_ref = refs[0:2], refs[2:4], refs[4], refs[5]
    to_rows, to_cols = refs[6:8], refs[8:10]
    if flat:
        v_ref, table_ref = refs[10:12]
    field, totals, *pairs, jac, sem = refs[-8:]
    xs, ys = pairs[0:2], pairs[2:4]
    kinds = jac.shape[0]
    fetches = [pltpu.make_async_copy(jac_hbm.at[t], jac.at[t], sem.at[t]) for t in range(kinds)]
    for fetch in fetches:
        fetch.start()
    if flat:
        make_plan(type_ref.shape[0], groups, faces_ref, type_ref, count_ref, table_ref)
    row_edges, col_edges = sides(side_ref, rows, cols)
    out_rows = [beyond(r, rows) for r in row_edges]
    out_cols = [beyond(c, cols) for c in col_edges]

    def cell_rows(cell):
        if isinstance(cell, int):
            return slice(cell * FR, (cell + 1) * FR)
        return pl.ds(pl.multiple_of(cell * FR, FR), FR)

    zero = jnp.zeros((FR, LANES), jnp.float32)
    field[0:FR, :] = zero
    if flat:
        sources = [(own_ref.at[r], (r + 1) * width + 1, 1, cols) for r in range(rows)]
        sources += [(row_refs[n], out_rows[n] * width + 1, 1, cols) for n in range(2)]
        sources += [(col_refs[n], width + out_cols[n], width, rows) for n in range(2)]
        for ref, first, step, many in sources:
            length = ref.shape[1]
            for a in range(FR):
                high = min(LANES * (a + 1), length)
                tile = ref[:, LANES * a : high].astype(jnp.float32)
                if high < LANES * (a + 1):
                    gap = jnp.zeros((many, LANES * (a + 1) - high), jnp.float32)
                    tile = jnp.concatenate([tile, gap], axis=1)
                field[pl.ds(first * FR + a, many, stride=step * FR), :] = tile
        for r in range(rows):
            for c in range(cols):
                v_ref[r * cols + c] = field[cell_rows((r + 1) * width + c + 1), :].astype(jnp.bfloat16)
    else:
        for r in range(rows):
            for c in range(cols):
                field[cell_rows((r + 1) * width + c + 1), :] = own_ref[r * cols + c].astype(jnp.float32)
        for n in range(2):
            for c in range(cols):
                field[cell_rows(out_rows[n] * width + c + 1), :] = row_refs[n][c].astype(jnp.float32)
            for r in range(rows):
                field[cell_rows((r + 1) * width + out_cols[n]), :] = col_refs[n][r].astype(jnp.float32)
    for cell in range((rows + 2) * width):
        totals[cell_rows(cell), :] = zero
    for y in ys:
        y[edge // 8 * 8 :, :] = jnp.zeros((y.shape[0] - edge // 8 * 8, LANES), jnp.float32)

    def gather(g, x):
        for f in range(6):
            at = [cell_rows(table_ref[(g * PACK + s) * 6 + f]) for s in range(PACK)]
            spread = swap_slots([field[at[s], :] for s in range(PACK)])
            for b in range(4):
                x[pl.ds(f * dofs + b, FR, stride=4), :] = spread[b]

    def multiply(g, x, y):
        kind = table_ref[groups * PACK * 6 + g]
        y[0:edge, :] = jnp.dot(
            jac[kind], x[0:edge, :].astype(jnp.bfloat16), preferred_element_type=jnp.float32
        )

    def scatter(g, y):
        for f in range(6):
            back = swap_slots([y[pl.ds(f * dofs + b, FR, stride=4), :] for b in range(4)])
            for s in range(PACK):
                at = cell_rows(table_ref[(g * PACK + s) * 6 + f])
                totals[at, :] = totals[at, :] + back[s]

    def pair(m, carry):
        gather(2 * m, xs[0])
        gather(2 * m + 1, xs[1])
        multiply(2 * m, xs[0], ys[0])
        multiply(2 * m + 1, xs[1], ys[1])
        scatter(2 * m, ys[0])
        scatter(2 * m + 1, ys[1])
        return carry

    done = jnp.int32(0)
    for t in range(kinds):
        fetches[t].wait()
        ready = table_ref[groups * (PACK * 6 + 1) + t]
        upto = (ready + 1) // 2 if t == kinds - 1 else ready // 2
        lax.fori_loop(done, upto, pair, jnp.int32(0))
        done = upto

    for r in range(rows):
        for c in range(cols):
            t_ref[r * cols + c] = totals[cell_rows((r + 1) * width + c + 1), :]
    for n in range(2):
        for c in range(cols):
            to_rows[n][c] = totals[cell_rows(out_rows[n] * width + c + 1), :].astype(jnp.bfloat16)
        for r in range(rows):
            to_cols[n][r] = totals[cell_rows((r + 1) * width + out_cols[n]), :].astype(jnp.bfloat16)


def combine(dims, side_ref, t_ref, rims, hold):
    rows, cols, dofs = dims
    row_edges, col_edges = sides(side_ref, rows, cols)
    for cell in range(rows * cols):
        hold[cell] = t_ref[cell]
    for n in range(2):
        for c in range(cols):
            cell = row_edges[n] * cols + c
            hold[cell] = hold[cell] + rims[n][c].astype(jnp.float32)
        for r in range(rows):
            cell = r * cols + col_edges[n]
            hold[cell] = hold[cell] + rims[2 + n][r].astype(jnp.float32)
    return row_edges, col_edges


def middle_kernel(dims, side_ref, t_ref, a_ref, b_ref, c_ref, d_ref, w_ref, *refs):
    rows, cols, dofs = dims
    hold = refs[-1]
    to_rows, to_cols = refs[0:2], refs[2:4]
    row_edges, col_edges = combine(dims, side_ref, t_ref, (a_ref, b_ref, c_ref, d_ref), hold)
    row = lax.broadcasted_iota(jnp.int32, (FR, LANES), 0)
    slot = lax.broadcasted_iota(jnp.int32, (FR, LANES), 1) // 32
    real = row * 4 + slot < dofs
    for cell in range(rows * cols):
        w_ref[cell] = jnp.where(real, hold[cell], 0.0).astype(jnp.bfloat16)
    for n in range(2):
        for c in range(cols):
            to_rows[n][c] = w_ref[row_edges[n] * cols + c]
        for r in range(rows):
            to_cols[n][r] = w_ref[r * cols + col_edges[n]]


def mail_kernel(dims, v_ref, w_ref, ids_ref, mail_ref):
    rows, cols, dofs = dims
    v = v_ref[...].reshape(rows * cols * FR, LANES)
    w = w_ref[...].reshape(rows * cols * FR, LANES)
    square = lax.dot_general(v, w, (((0,), (0,)), ((), ())), preferred_element_type=jnp.float32)
    side = lax.broadcasted_iota(jnp.int32, (LANES, LANES), 1) // 32
    diagonal = lax.broadcasted_iota(jnp.int32, (LANES, LANES), 0) // 32 == side
    square = jnp.where(diagonal, square, 0.0)
    local = square[0:32] + square[32:64] + square[64:96] + square[96:128]
    local = local + pltpu.roll(local, 64, 1)
    local = (local + pltpu.roll(local, 32, 1)) * (1.0 / math.sqrt(rows * cols * dofs))
    local = jnp.where(diagonal, jnp.concatenate([local] * 4, axis=0), 0.0)
    owners = mail_ref.shape[0]
    ids = ids_ref[...]
    owner = lax.broadcasted_iota(jnp.int32, (owners, LANES), 0)
    vertex = 4 * owner + lax.broadcasted_iota(jnp.int32, (owners, LANES), 1) // 32
    place = (vertex == ids).astype(jnp.bfloat16)
    high = local.astype(jnp.bfloat16)
    low = (local - high.astype(jnp.float32)).astype(jnp.bfloat16)
    mail_ref[:, 0, :] = jnp.dot(place, high, preferred_element_type=jnp.float32) + jnp.dot(
        place, low, preferred_element_type=jnp.float32
    )
    mail_ref[:, 1, :] = jnp.broadcast_to(ids.astype(jnp.float32), (owners, LANES))


def expand_kernel(mail_ref, out_ref, turned_ref, where_ref, flat_ref, at_ref, hot_ref):
    senders = mail_ref.shape[0]
    vertices = out_ref.shape[2]
    parts = (vertices + LANES - 1) // LANES
    low = lax.broadcasted_iota(jnp.int32, (LANES, senders), 0)
    turned_ref[...] = mail_ref[:, 0, :].T
    where_ref[...] = mail_ref[:, 1, :].T.astype(jnp.int32)
    for s in range(32):
        part = slice(s * senders, (s + 1) * senders)
        flat_ref[:, part] = turned_ref[pl.ds(s, 4, stride=32), :]
        ids = where_ref[s : s + 1, :]
        at_ref[:, part] = ids // LANES
        hot_ref[:, part] = (ids % LANES == low).astype(jnp.bfloat16)
    values = flat_ref[...]
    high = values.astype(jnp.bfloat16).astype(jnp.float32)
    block = at_ref[...]
    left = [
        jnp.where(block == h, piece, 0.0) for piece in (high, values - high) for h in range(parts)
    ]
    left = jnp.concatenate(left, axis=0).astype(jnp.bfloat16)
    wide = lax.dot_general(
        left, hot_ref[...], (((1,), (1,)), ((), ())), preferred_element_type=jnp.float32
    )
    for h in range(parts):
        total = wide[4 * h : 4 * h + 4] + wide[4 * (parts + h) : 4 * (parts + h) + 4]
        high = min(LANES * (h + 1), vertices)
        for j in range(out_ref.shape[0]):
            out_ref[j, :, LANES * h : high] = total[:, 0 : high - LANES * h]


def last_kernel(dims, side_ref, t_ref, a_ref, b_ref, c_ref, d_ref, out_ref, sums, hold):
    rows, cols, dofs = dims
    length = out_ref.shape[2]
    combine(dims, side_ref, t_ref, (a_ref, b_ref, c_ref, d_ref), sums)
    for r in range(rows):
        for c in range(cols):
            hold[pl.ds(r * FR * cols + c, FR, stride=cols), :] = sums[r * cols + c]
    for r in range(rows):
        for a in range(FR):
            high = min(LANES * (a + 1), length)
            start = (r * FR + a) * cols
            tile = hold[start : start + cols, 0 : high - LANES * a]
            out_ref[r, :, LANES * a : high] = tile.astype(jnp.bfloat16)


VM = pl.BlockSpec(memory_space=pltpu.VMEM)
SM = pl.BlockSpec(memory_space=pltpu.SMEM)
HBM = pl.BlockSpec(memory_space=pltpu.HBM)


def struct(shape, dtype=jnp.bfloat16):
    return jax.ShapeDtypeStruct(shape, dtype)


def rim_structs(rows, cols):
    return (
        struct((cols, FR, LANES)),
        struct((cols, FR, LANES)),
        struct((rows, FR, LANES)),
        struct((rows, FR, LANES)),
    )


def apply(flat, dims, side, scalars, own, rims, jacobians):
    rows, cols, dofs = dims
    cells = rows * cols
    slots = scalars[1].shape[0] if flat else 0
    groups = (slots + 3 * 4) // PACK // 2 * 2 if flat else (scalars[0].shape[0] - jacobians.shape[0]) // (PACK * 6 + 1)
    out = (struct((cells, FR, LANES), jnp.float32),) + rim_structs(rows, cols)
    places = (VM,) * 5
    if flat:
        out += (struct((cells, FR, LANES)), struct((groups * (PACK * 6 + 1) + jacobians.shape[0],), jnp.int32))
        places += (VM, SM)
    area = (rows + 2) * (cols + 2) * FR
    flops = 2**34
    moved = jacobians.size * 2 + cells * FR * LANES * 6
    return pl.pallas_call(
        functools.partial(apply_kernel, flat, dims, groups),
        out_shape=out,
        in_specs=[SM] * (1 + len(scalars)) + [VM] * 5 + [HBM],
        out_specs=places,
        scratch_shapes=[
            pltpu.VMEM((area, LANES), jnp.float32),
            pltpu.VMEM((area, LANES), jnp.float32),
            *[pltpu.VMEM((6 * dofs + 10, LANES), jnp.float32)] * 4,
            pltpu.VMEM(jacobians.shape, jnp.bfloat16),
            pltpu.SemaphoreType.DMA((jacobians.shape[0],)),
        ],
        compiler_params=pltpu.CompilerParams(vmem_limit_bytes=VMEM_LIMIT),
        cost_estimate=pl.CostEstimate(flops=flops, bytes_accessed=moved, transcendentals=0),
        name="apply_flat" if flat else "apply_tiles",
    )(side, *scalars, own, *rims, jacobians)


def middle(dims, side, total, rims):
    rows, cols, dofs = dims
    cells = rows * cols
    return pl.pallas_call(
        functools.partial(middle_kernel, dims),
        out_shape=(struct((cells, FR, LANES)),) + rim_structs(rows, cols),
        in_specs=[SM] + [VM] * 5,
        out_specs=(VM,) * 5,
        scratch_shapes=[pltpu.VMEM((cells, FR, LANES), jnp.float32)],
        compiler_params=pltpu.CompilerParams(vmem_limit_bytes=VMEM_LIMIT),
        name="middle",
    )(side, total, *rims)


def make_mail(dims, tiles, first, ids, owners):
    return pl.pallas_call(
        functools.partial(mail_kernel, dims),
        out_shape=struct((owners, 2, LANES), jnp.float32),
        in_specs=[VM] * 3,
        out_specs=VM,
        compiler_params=pltpu.CompilerParams(vmem_limit_bytes=VMEM_LIMIT),
        cost_estimate=pl.CostEstimate(flops=2**30, bytes_accessed=2**20, transcendentals=0),
        name="mail",
    )(tiles, first, ids)


def expand(mail, narrow, vertex_total):
    owned = vertex_total // mail.shape[0]
    return pl.pallas_call(
        expand_kernel,
        out_shape=struct((narrow, owned, vertex_total), jnp.float32),
        in_specs=[VM],
        out_specs=VM,
        scratch_shapes=[
            pltpu.VMEM((LANES, mail.shape[0]), jnp.float32),
            pltpu.VMEM((LANES, mail.shape[0]), jnp.int32),
            pltpu.VMEM((owned, 32 * mail.shape[0]), jnp.float32),
            pltpu.VMEM((1, 32 * mail.shape[0]), jnp.int32),
            pltpu.VMEM((LANES, 32 * mail.shape[0]), jnp.bfloat16),
        ],
        compiler_params=pltpu.CompilerParams(vmem_limit_bytes=VMEM_LIMIT),
        cost_estimate=pl.CostEstimate(flops=2**30, bytes_accessed=2**18, transcendentals=0),
        name="expand",
    )(mail)


def last(dims, side, total, rims, length):
    rows, cols, dofs = dims
    cells = rows * cols
    return pl.pallas_call(
        functools.partial(last_kernel, dims),
        out_shape=struct((rows, cols, length)),
        in_specs=[SM] + [VM] * 5,
        out_specs=VM,
        scratch_shapes=[
            pltpu.VMEM((cells, FR, LANES), jnp.float32),
            pltpu.VMEM((cells * FR, LANES), jnp.float32),
        ],
        compiler_params=pltpu.CompilerParams(vmem_limit_bytes=VMEM_LIMIT),
        cost_estimate=pl.CostEstimate(flops=2**34, bytes_accessed=2**20, transcendentals=0),
        name="last",
    )(side, total, *rims)


def exchange(row_second, row_first, col_first, col_second):
    def swap(value, axis, start):
        peers = lax.axis_size(axis)
        pairs = [(i, i + 1) for i in range(start, peers - 1, 2)]
        return lax.ppermute(value, axis, pairs + [(j, i) for i, j in pairs])

    return (
        swap(row_second, "sub", 1),
        swap(row_first, "sub", 0),
        swap(col_first, "slab", 0),
        swap(col_second, "slab", 1),
    )


def body(coarse_basis, jacobians, element_faces, element_type, element_count, vertex_ids):
    rows, cols, length = coarse_basis.shape
    dofs = jacobians.shape[1] // 6
    dims = (rows, cols, dofs)
    owners, narrow = lax.axis_size("sub"), lax.axis_size("slab")
    ids = jnp.tile(vertex_ids, (1, 4))
    odd_row, odd_col = lax.axis_index("sub") & 1, lax.axis_index("slab") & 1
    side = jnp.stack([odd_row, odd_col])

    ends = coarse_basis[0], coarse_basis[rows - 1], coarse_basis[:, 0], coarse_basis[:, cols - 1]
    rims = exchange(
        jnp.where(odd_row == 1, ends[1], ends[0]),
        jnp.where(odd_row == 1, ends[0], ends[1]),
        jnp.where(odd_col == 1, ends[2], ends[3]),
        jnp.where(odd_col == 1, ends[3], ends[2]),
    )
    scalars = (element_faces.T, element_type, element_count)
    total, *sent, tiles, table = apply(True, dims, side, scalars, coarse_basis, rims, jacobians)
    first, *halo = middle(dims, side, total, exchange(*sent))
    rims = exchange(*halo)
    tiles, unused = lax.optimization_barrier((tiles, rims[0]))
    mail = lax.all_to_all(make_mail(dims, tiles, first, ids, owners), "sub", 0, 0)
    total, *sent = apply(False, dims, side, (table,), first, rims, jacobians)
    rims = exchange(*sent)
    mail, unused = lax.optimization_barrier((mail, rims[0]))
    parts = lax.all_to_all(expand(mail, narrow, rows * owners), "slab", 0, 0)
    second_image = last(dims, side, total, rims, length)
    return second_image, parts.sum(0)


def solution(mesh):
    return jax.shard_map(
        body,
        mesh=mesh,
        in_specs=(
            P("sub", "slab", None),
            P(),
            P(("sub", "slab"), None),
            P(("sub", "slab")),
            P(("sub", "slab")),
            P(("sub", "slab"), None),
        ),
        out_specs=(P("sub", "slab", None), P("sub", None)),
        check_vma=False,
    )
```

```python
import functools
import math

import jax
import jax.numpy as jnp
from jax import lax
from jax.experimental import pallas as pl
from jax.experimental.pallas import tpu as pltpu
from jax.sharding import PartitionSpec as P

FR = 32
LANES = 128
PACK = 4
VMEM_LIMIT = 50 * 1024 * 1024


def swap_slots(values):
    slot = lax.broadcasted_iota(jnp.int32, values[0].shape, 1) // 32
    upper = slot >= 2
    odd = slot % 2 == 1
    a, b, c, d = values
    a, c = jnp.where(upper, pltpu.roll(c, 64, 1), a), jnp.where(upper, c, pltpu.roll(a, 64, 1))
    b, d = jnp.where(upper, pltpu.roll(d, 64, 1), b), jnp.where(upper, d, pltpu.roll(b, 64, 1))
    a, b = jnp.where(odd, pltpu.roll(b, 32, 1), a), jnp.where(odd, b, pltpu.roll(a, 96, 1))
    c, d = jnp.where(odd, pltpu.roll(d, 32, 1), c), jnp.where(odd, d, pltpu.roll(c, 96, 1))
    return [a, b, c, d]


def make_plan(slots, groups, faces_ref, type_ref, count_ref, table_ref):
    kind_at = groups * PACK * 6
    for i in range(kind_at):
        table_ref[i] = 0
    count = count_ref[0]
    kinds = 4

    def tally(slot, sizes):
        live = slot < count
        return tuple(
            size + (live & (type_ref[slot] == kind)).astype(jnp.int32)
            for kind, size in enumerate(sizes)
        )

    sizes = lax.fori_loop(0, slots, tally, (jnp.int32(0),) * kinds)
    firsts, place = [], jnp.int32(0)
    for kind, size in enumerate(sizes):
        firsts.append(place)
        place = place + (size + PACK - 1) // PACK * PACK
        table_ref[kind_at + groups + kind] = place // PACK

    def put(slot, nexts):
        kind = type_ref[slot]
        position = nexts[kinds - 1]
        for other in range(kinds - 1):
            position = jnp.where(kind == other, nexts[other], position)
        table_ref[kind_at + position // PACK] = kind
        for f in range(6):
            table_ref[position * 6 + f] = faces_ref[f, slot]
        return tuple(at + (kind == other).astype(jnp.int32) for other, at in enumerate(nexts))

    lax.fori_loop(0, count, put, tuple(firsts))


def sides(side_ref, rows, cols):
    odd_row, odd_col = side_ref[0] == 1, side_ref[1] == 1
    first_row = jnp.where(odd_row, 0, rows - 1)
    first_col = jnp.where(odd_col, 0, cols - 1)
    return (rows - 1 - first_row, first_row), (first_col, cols - 1 - first_col)


def beyond(edge, length):
    return jnp.where(edge == 0, 0, length + 1)


def near_views(side_ref, rows, refs):
    far_ref, block_ref, second_ref = refs
    me = side_ref[0] * 2 + side_ref[1]
    row = jnp.where(side_ref[0] == 1, me - 2, me + 2)
    col = jnp.where(side_ref[1] == 1, me - 1, me + 1)
    return (far_ref, block_ref.at[row]), (block_ref.at[col], second_ref)


def apply_kernel(flat, dims, groups, *refs):
    rows, cols, dofs = dims
    edge = 6 * dofs
    width = cols + 2
    if flat:
        side_ref, faces_ref, type_ref, count_ref, own_ref, *refs = refs
    else:
        side_ref, table_ref, own_ref, *refs = refs
    if flat:
        row_refs, col_refs = refs[0:2], refs[2:4]
        v_ref, table_ref = refs[9:11]
        jac_hbm, t_ref, *sent = refs[4:9]
    else:
        row_refs, col_refs = near_views(side_ref, rows, refs[0:3])
        jac_hbm, t_ref, *sent = refs[3:8]
    sent[1][...] = jnp.zeros_like(sent[1])
    to_rows, to_cols = near_views(side_ref, rows, sent)
    field, totals, *pairs, jac, sem = refs[-8:]
    xs, ys = pairs[0:2], pairs[2:4]
    kinds = jac.shape[0]
    fetches = [pltpu.make_async_copy(jac_hbm.at[t], jac.at[t], sem.at[t]) for t in range(kinds)]
    for fetch in fetches:
        fetch.start()
    if flat:
        make_plan(type_ref.shape[0], groups, faces_ref, type_ref, count_ref, table_ref)
    row_edges, col_edges = sides(side_ref, rows, cols)
    out_rows = [beyond(r, rows) for r in row_edges]
    out_cols = [beyond(c, cols) for c in col_edges]

    def cell_rows(cell):
        if isinstance(cell, int):
            return slice(cell * FR, (cell + 1) * FR)
        return pl.ds(pl.multiple_of(cell * FR, FR), FR)

    zero = jnp.zeros((FR, LANES), jnp.float32)
    field[0:FR, :] = zero
    if flat:
        sources = [(own_ref.at[r], (r + 1) * width + 1, 1, cols) for r in range(rows)]
        sources += [(row_refs[n], out_rows[n] * width + 1, 1, cols) for n in range(2)]
        sources += [(col_refs[n], width + out_cols[n], width, rows) for n in range(2)]
        for ref, first, step, many in sources:
            length = ref.shape[1]
            for a in range(FR):
                high = min(LANES * (a + 1), length)
                tile = ref[:, LANES * a : high].astype(jnp.float32)
                if high < LANES * (a + 1):
                    gap = jnp.zeros((many, LANES * (a + 1) - high), jnp.float32)
                    tile = jnp.concatenate([tile, gap], axis=1)
                field[pl.ds(first * FR + a, many, stride=step * FR), :] = tile
        for r in range(rows):
            for c in range(cols):
                v_ref[r * cols + c] = field[cell_rows((r + 1) * width + c + 1), :].astype(jnp.bfloat16)
    else:
        for r in range(rows):
            for c in range(cols):
                field[cell_rows((r + 1) * width + c + 1), :] = own_ref[r * cols + c].astype(jnp.float32)
        for n in range(2):
            for c in range(cols):
                field[cell_rows(out_rows[n] * width + c + 1), :] = row_refs[n][c].astype(jnp.float32)
            for r in range(rows):
                field[cell_rows((r + 1) * width + out_cols[n]), :] = col_refs[n][r].astype(jnp.float32)
    for cell in range((rows + 2) * width):
        totals[cell_rows(cell), :] = zero
    for y in ys:
        y[edge // 8 * 8 :, :] = jnp.zeros((y.shape[0] - edge // 8 * 8, LANES), jnp.float32)

    def gather(g, x):
        for f in range(6):
            at = [cell_rows(table_ref[(g * PACK + s) * 6 + f]) for s in range(PACK)]
            spread = swap_slots([field[at[s], :] for s in range(PACK)])
            for b in range(4):
                x[pl.ds(f * dofs + b, FR, stride=4), :] = spread[b]

    def multiply(g, x, y):
        kind = table_ref[groups * PACK * 6 + g]
        y[0:edge, :] = jnp.dot(
            jac[kind], x[0:edge, :].astype(jnp.bfloat16), preferred_element_type=jnp.float32
        )

    def scatter(g, y):
        for f in range(6):
            back = swap_slots([y[pl.ds(f * dofs + b, FR, stride=4), :] for b in range(4)])
            for s in range(PACK):
                at = cell_rows(table_ref[(g * PACK + s) * 6 + f])
                totals[at, :] = totals[at, :] + back[s]

    def pair(m, carry):
        gather(2 * m, xs[0])
        gather(2 * m + 1, xs[1])
        multiply(2 * m, xs[0], ys[0])
        multiply(2 * m + 1, xs[1], ys[1])
        scatter(2 * m, ys[0])
        scatter(2 * m + 1, ys[1])
        return carry

    done = jnp.int32(0)
    for t in range(kinds):
        fetches[t].wait()
        ready = table_ref[groups * (PACK * 6 + 1) + t]
        upto = (ready + 1) // 2 if t == kinds - 1 else ready // 2
        lax.fori_loop(done, upto, pair, jnp.int32(0))
        done = upto

    for r in range(rows):
        for c in range(cols):
            t_ref[r * cols + c] = totals[cell_rows((r + 1) * width + c + 1), :]
    for n in range(2):
        for c in range(cols):
            to_rows[n][c] = totals[cell_rows(out_rows[n] * width + c + 1), :].astype(jnp.bfloat16)
        for r in range(rows):
            to_cols[n][r] = totals[cell_rows((r + 1) * width + out_cols[n]), :].astype(jnp.bfloat16)


def combine(dims, side_ref, t_ref, refs, hold):
    rows, cols, dofs = dims
    row_refs, col_refs = near_views(side_ref, rows, refs)
    row_edges, col_edges = sides(side_ref, rows, cols)
    for cell in range(rows * cols):
        hold[cell] = t_ref[cell]
    for n in range(2):
        for c in range(cols):
            cell = row_edges[n] * cols + c
            hold[cell] = hold[cell] + row_refs[n][c].astype(jnp.float32)
        for r in range(rows):
            cell = r * cols + col_edges[n]
            hold[cell] = hold[cell] + col_refs[n][r].astype(jnp.float32)
    return row_edges, col_edges


def middle_kernel(dims, side_ref, t_ref, a_ref, b_ref, c_ref, w_ref, *refs):
    rows, cols, dofs = dims
    hold = refs[-1]
    refs[1][...] = jnp.zeros_like(refs[1])
    to_rows, to_cols = near_views(side_ref, rows, refs[0:3])
    row_edges, col_edges = combine(dims, side_ref, t_ref, (a_ref, b_ref, c_ref), hold)
    row = lax.broadcasted_iota(jnp.int32, (FR, LANES), 0)
    slot = lax.broadcasted_iota(jnp.int32, (FR, LANES), 1) // 32
    real = row * 4 + slot < dofs
    for cell in range(rows * cols):
        w_ref[cell] = jnp.where(real, hold[cell], 0.0).astype(jnp.bfloat16)
    for n in range(2):
        for c in range(cols):
            to_rows[n][c] = w_ref[row_edges[n] * cols + c]
        for r in range(rows):
            to_cols[n][r] = w_ref[r * cols + col_edges[n]]


def mail_kernel(dims, v_ref, w_ref, ids_ref, mail_ref):
    rows, cols, dofs = dims
    v = v_ref[...].reshape(rows * cols * FR, LANES)
    w = w_ref[...].reshape(rows * cols * FR, LANES)
    square = lax.dot_general(v, w, (((0,), (0,)), ((), ())), preferred_element_type=jnp.float32)
    side = lax.broadcasted_iota(jnp.int32, (LANES, LANES), 1) // 32
    diagonal = lax.broadcasted_iota(jnp.int32, (LANES, LANES), 0) // 32 == side
    square = jnp.where(diagonal, square, 0.0)
    local = square[0:32] + square[32:64] + square[64:96] + square[96:128]
    local = local + pltpu.roll(local, 64, 1)
    local = (local + pltpu.roll(local, 32, 1)) * (1.0 / math.sqrt(rows * cols * dofs))
    local = jnp.where(diagonal, jnp.concatenate([local] * 4, axis=0), 0.0)
    owners = mail_ref.shape[0]
    ids = ids_ref[...]
    owner = lax.broadcasted_iota(jnp.int32, (owners, LANES), 0)
    vertex = 4 * owner + lax.broadcasted_iota(jnp.int32, (owners, LANES), 1) // 32
    place = (vertex == ids).astype(jnp.bfloat16)
    high = local.astype(jnp.bfloat16)
    low = (local - high.astype(jnp.float32)).astype(jnp.bfloat16)
    mail_ref[:, 0, :] = jnp.dot(place, high, preferred_element_type=jnp.float32) + jnp.dot(
        place, low, preferred_element_type=jnp.float32
    )
    mail_ref[:, 1, :] = jnp.broadcast_to(ids.astype(jnp.float32), (owners, LANES))


def expand_kernel(mail_ref, out_ref, turned_ref, where_ref, flat_ref, at_ref, hot_ref):
    senders = mail_ref.shape[0]
    vertices = out_ref.shape[2]
    parts = (vertices + LANES - 1) // LANES
    low = lax.broadcasted_iota(jnp.int32, (LANES, senders), 0)
    turned_ref[...] = mail_ref[:, 0, :].T
    where_ref[...] = mail_ref[:, 1, :].T.astype(jnp.int32)
    for s in range(32):
        part = slice(s * senders, (s + 1) * senders)
        flat_ref[:, part] = turned_ref[pl.ds(s, 4, stride=32), :]
        ids = where_ref[s : s + 1, :]
        at_ref[:, part] = ids // LANES
        hot_ref[:, part] = (ids % LANES == low).astype(jnp.bfloat16)
    values = flat_ref[...]
    high = values.astype(jnp.bfloat16).astype(jnp.float32)
    block = at_ref[...]
    left = [
        jnp.where(block == h, piece, 0.0) for piece in (high, values - high) for h in range(parts)
    ]
    left = jnp.concatenate(left, axis=0).astype(jnp.bfloat16)
    wide = lax.dot_general(
        left, hot_ref[...], (((1,), (1,)), ((), ())), preferred_element_type=jnp.float32
    )
    for h in range(parts):
        total = wide[4 * h : 4 * h + 4] + wide[4 * (parts + h) : 4 * (parts + h) + 4]
        high = min(LANES * (h + 1), vertices)
        for j in range(out_ref.shape[0]):
            out_ref[j, :, LANES * h : high] = total[:, 0 : high - LANES * h]


def last_kernel(dims, side_ref, t_ref, a_ref, b_ref, c_ref, out_ref, sums, hold):
    rows, cols, dofs = dims
    length = out_ref.shape[2]
    combine(dims, side_ref, t_ref, (a_ref, b_ref, c_ref), sums)
    for r in range(rows):
        for c in range(cols):
            hold[pl.ds(r * FR * cols + c, FR, stride=cols), :] = sums[r * cols + c]
    for r in range(rows):
        for a in range(FR):
            high = min(LANES * (a + 1), length)
            start = (r * FR + a) * cols
            tile = hold[start : start + cols, 0 : high - LANES * a]
            out_ref[r, :, LANES * a : high] = tile.astype(jnp.bfloat16)


VM = pl.BlockSpec(memory_space=pltpu.VMEM)
SM = pl.BlockSpec(memory_space=pltpu.SMEM)
HBM = pl.BlockSpec(memory_space=pltpu.HBM)


def struct(shape, dtype=jnp.bfloat16):
    return jax.ShapeDtypeStruct(shape, dtype)


def rim_structs(rows, cols):
    return (
        struct((cols, FR, LANES)),
        struct((4, max(rows, cols), FR, LANES)),
        struct((rows, FR, LANES)),
    )


def apply(flat, dims, side, scalars, own, rims, jacobians):
    rows, cols, dofs = dims
    cells = rows * cols
    slots = scalars[1].shape[0] if flat else 0
    groups = (slots + 3 * 4) // PACK // 2 * 2 if flat else (scalars[0].shape[0] - jacobians.shape[0]) // (PACK * 6 + 1)
    out = (struct((cells, FR, LANES), jnp.float32),) + rim_structs(rows, cols)
    places = (VM,) * 4
    if flat:
        out += (struct((cells, FR, LANES)), struct((groups * (PACK * 6 + 1) + jacobians.shape[0],), jnp.int32))
        places += (VM, SM)
    area = (rows + 2) * (cols + 2) * FR
    flops = 2**34
    moved = jacobians.size * 2 + cells * FR * LANES * 6
    return pl.pallas_call(
        functools.partial(apply_kernel, flat, dims, groups),
        out_shape=out,
        in_specs=[SM] * (1 + len(scalars)) + [VM] * (1 + len(rims)) + [HBM],
        out_specs=places,
        scratch_shapes=[
            pltpu.VMEM((area, LANES), jnp.float32),
            pltpu.VMEM((area, LANES), jnp.float32),
            *[pltpu.VMEM((6 * dofs + 10, LANES), jnp.float32)] * 4,
            pltpu.VMEM(jacobians.shape, jnp.bfloat16),
            pltpu.SemaphoreType.DMA((jacobians.shape[0],)),
        ],
        compiler_params=pltpu.CompilerParams(vmem_limit_bytes=VMEM_LIMIT),
        cost_estimate=pl.CostEstimate(flops=flops, bytes_accessed=moved, transcendentals=0),
        name="apply_flat" if flat else "apply_tiles",
    )(side, *scalars, own, *rims, jacobians)


def middle(dims, side, total, rims):
    rows, cols, dofs = dims
    cells = rows * cols
    return pl.pallas_call(
        functools.partial(middle_kernel, dims),
        out_shape=(struct((cells, FR, LANES)),) + rim_structs(rows, cols),
        in_specs=[SM] + [VM] * 4,
        out_specs=(VM,) * 4,
        scratch_shapes=[pltpu.VMEM((cells, FR, LANES), jnp.float32)],
        compiler_params=pltpu.CompilerParams(vmem_limit_bytes=VMEM_LIMIT),
        name="middle",
    )(side, total, *rims)


def make_mail(dims, tiles, first, ids, owners):
    return pl.pallas_call(
        functools.partial(mail_kernel, dims),
        out_shape=struct((owners, 2, LANES), jnp.float32),
        in_specs=[VM] * 3,
        out_specs=VM,
        compiler_params=pltpu.CompilerParams(vmem_limit_bytes=VMEM_LIMIT),
        cost_estimate=pl.CostEstimate(flops=2**30, bytes_accessed=2**20, transcendentals=0),
        name="mail",
    )(tiles, first, ids)


def expand(mail, narrow, vertex_total):
    owned = vertex_total // mail.shape[0]
    return pl.pallas_call(
        expand_kernel,
        out_shape=struct((narrow, owned, vertex_total), jnp.float32),
        in_specs=[VM],
        out_specs=VM,
        scratch_shapes=[
            pltpu.VMEM((LANES, mail.shape[0]), jnp.float32),
            pltpu.VMEM((LANES, mail.shape[0]), jnp.int32),
            pltpu.VMEM((owned, 32 * mail.shape[0]), jnp.float32),
            pltpu.VMEM((1, 32 * mail.shape[0]), jnp.int32),
            pltpu.VMEM((LANES, 32 * mail.shape[0]), jnp.bfloat16),
        ],
        compiler_params=pltpu.CompilerParams(vmem_limit_bytes=VMEM_LIMIT),
        cost_estimate=pl.CostEstimate(flops=2**30, bytes_accessed=2**18, transcendentals=0),
        name="expand",
    )(mail)


def last(dims, side, total, rims, length):
    rows, cols, dofs = dims
    cells = rows * cols
    return pl.pallas_call(
        functools.partial(last_kernel, dims),
        out_shape=struct((rows, cols, length)),
        in_specs=[SM] + [VM] * 4,
        out_specs=VM,
        scratch_shapes=[
            pltpu.VMEM((cells, FR, LANES), jnp.float32),
            pltpu.VMEM((cells * FR, LANES), jnp.float32),
        ],
        compiler_params=pltpu.CompilerParams(vmem_limit_bytes=VMEM_LIMIT),
        cost_estimate=pl.CostEstimate(flops=2**34, bytes_accessed=2**20, transcendentals=0),
        name="last",
    )(side, total, *rims)


def swap(value, axis, start):
    peers = lax.axis_size(axis)
    pairs = [(i, i + 1) for i in range(start, peers - 1, 2)]
    return lax.ppermute(value, axis, pairs + [(j, i) for i, j in pairs])


def exchange(far, block, col_second):
    wide, narrow = lax.axis_size("sub"), lax.axis_size("slab")
    blocks = [
        [(i + di) * narrow + j + dj for di in range(2) for dj in range(2)]
        for i in range(0, wide, 2)
        for j in range(0, narrow, 2)
    ]
    return (
        swap(far, "sub", 1),
        lax.all_to_all(block, ("sub", "slab"), 0, 0, axis_index_groups=blocks),
        swap(col_second, "slab", 1),
    )


def body(coarse_basis, jacobians, element_faces, element_type, element_count, vertex_ids):
    rows, cols, length = coarse_basis.shape
    dofs = jacobians.shape[1] // 6
    dims = (rows, cols, dofs)
    owners, narrow = lax.axis_size("sub"), lax.axis_size("slab")
    ids = jnp.tile(vertex_ids, (1, 4))
    odd_row, odd_col = lax.axis_index("sub") & 1, lax.axis_index("slab") & 1
    side = jnp.stack([odd_row, odd_col])

    ends = coarse_basis[0], coarse_basis[rows - 1], coarse_basis[:, 0], coarse_basis[:, cols - 1]
    rims = (
        swap(jnp.where(odd_row == 1, ends[1], ends[0]), "sub", 1),
        swap(jnp.where(odd_row == 1, ends[0], ends[1]), "sub", 0),
        swap(jnp.where(odd_col == 1, ends[2], ends[3]), "slab", 0),
        swap(jnp.where(odd_col == 1, ends[3], ends[2]), "slab", 1),
    )
    scalars = (element_faces.T, element_type, element_count)
    total, *sent, tiles, table = apply(True, dims, side, scalars, coarse_basis, rims, jacobians)
    first, *halo = middle(dims, side, total, exchange(*sent))
    rims = exchange(*halo)
    tiles, unused = lax.optimization_barrier((tiles, rims[0]))
    mail = lax.all_to_all(make_mail(dims, tiles, first, ids, owners), "sub", 0, 0)
    total, *sent = apply(False, dims, side, (table,), first, rims, jacobians)
    rims = exchange(*sent)
    mail, unused = lax.optimization_barrier((mail, rims[0]))
    parts = lax.all_to_all(expand(mail, narrow, rows * owners), "slab", 0, 0)
    second_image = last(dims, side, total, rims, length)
    return second_image, parts.sum(0)


def solution(mesh):
    return jax.shard_map(
        body,
        mesh=mesh,
        in_specs=(
            P("sub", "slab", None),
            P(),
            P(("sub", "slab"), None),
            P(("sub", "slab")),
            P(("sub", "slab")),
            P(("sub", "slab"), None),
        ),
        out_specs=(P("sub", "slab", None), P("sub", None)),
        check_vma=False,
    )
```

```python
import functools
import math

import jax
import jax.numpy as jnp
from jax import lax
from jax.experimental import pallas as pl
from jax.experimental.pallas import tpu as pltpu
from jax.sharding import PartitionSpec as P

FR = 32
LANES = 128
PACK = 4
VMEM_LIMIT = 50 * 1024 * 1024


def swap_slots(values):
    slot = lax.broadcasted_iota(jnp.int32, values[0].shape, 1) // 32
    upper = slot >= 2
    odd = slot % 2 == 1
    a, b, c, d = values
    a, c = jnp.where(upper, pltpu.roll(c, 64, 1), a), jnp.where(upper, c, pltpu.roll(a, 64, 1))
    b, d = jnp.where(upper, pltpu.roll(d, 64, 1), b), jnp.where(upper, d, pltpu.roll(b, 64, 1))
    a, b = jnp.where(odd, pltpu.roll(b, 32, 1), a), jnp.where(odd, b, pltpu.roll(a, 96, 1))
    c, d = jnp.where(odd, pltpu.roll(d, 32, 1), c), jnp.where(odd, d, pltpu.roll(c, 96, 1))
    return [a, b, c, d]


def make_plan(slots, groups, faces_ref, type_ref, count_ref, table_ref):
    kind_at = groups * PACK * 6
    for i in range(kind_at):
        table_ref[i] = 0
    count = count_ref[0]
    kinds = 4

    def tally(slot, sizes):
        live = slot < count
        return tuple(
            size + (live & (type_ref[slot] == kind)).astype(jnp.int32)
            for kind, size in enumerate(sizes)
        )

    sizes = lax.fori_loop(0, slots, tally, (jnp.int32(0),) * kinds)
    firsts, place = [], jnp.int32(0)
    for kind, size in enumerate(sizes):
        firsts.append(place)
        place = place + (size + PACK - 1) // PACK * PACK
        table_ref[kind_at + groups + kind] = place // PACK

    def put(slot, nexts):
        kind = type_ref[slot]
        position = nexts[kinds - 1]
        for other in range(kinds - 1):
            position = jnp.where(kind == other, nexts[other], position)
        table_ref[kind_at + position // PACK] = kind
        for f in range(6):
            table_ref[position * 6 + f] = faces_ref[f, slot]
        return tuple(at + (kind == other).astype(jnp.int32) for other, at in enumerate(nexts))

    lax.fori_loop(0, count, put, tuple(firsts))


def sides(side_ref, rows, cols):
    odd_row, odd_col = side_ref[0] == 1, side_ref[1] == 1
    first_row = jnp.where(odd_row, 0, rows - 1)
    first_col = jnp.where(odd_col, 0, cols - 1)
    return (rows - 1 - first_row, first_row), (first_col, cols - 1 - first_col)


def beyond(edge, length):
    return jnp.where(edge == 0, 0, length + 1)


def apply_kernel(flat, dims, groups, *refs):
    rows, cols, dofs = dims
    edge = 6 * dofs
    width = cols + 2
    if flat:
        side_ref, faces_ref, type_ref, count_ref, own_ref, *refs = refs
    else:
        side_ref, table_ref, own_ref, *refs = refs
    row_refs, col_refs, jac_hbm, t_ref = refs[0:2], refs[2:4], refs[4], refs[5]
    to_rows, to_cols = refs[6:8], refs[8:10]
    if flat:
        v_ref, table_ref = refs[10:12]
    field, totals, *pairs, jac, sem = refs[-8:]
    xs, ys = pairs[0:2], pairs[2:4]
    kinds = jac.shape[0]
    fetches = [pltpu.make_async_copy(jac_hbm.at[t], jac.at[t], sem.at[t]) for t in range(kinds)]
    for fetch in fetches:
        fetch.start()
    if flat:
        make_plan(type_ref.shape[0], groups, faces_ref, type_ref, count_ref, table_ref)
    row_edges, col_edges = sides(side_ref, rows, cols)
    out_rows = [beyond(r, rows) for r in row_edges]
    out_cols = [beyond(c, cols) for c in col_edges]

    def cell_rows(cell):
        if isinstance(cell, int):
            return slice(cell * FR, (cell + 1) * FR)
        return pl.ds(pl.multiple_of(cell * FR, FR), FR)

    zero = jnp.zeros((FR, LANES), jnp.float32)
    field[0:FR, :] = zero
    if flat:
        sources = [(own_ref.at[r], (r + 1) * width + 1, 1, cols) for r in range(rows)]
        sources += [(row_refs[n], out_rows[n] * width + 1, 1, cols) for n in range(2)]
        sources += [(col_refs[n], width + out_cols[n], width, rows) for n in range(2)]
        for ref, first, step, many in sources:
            length = ref.shape[1]
            for a in range(FR):
                high = min(LANES * (a + 1), length)
                tile = ref[:, LANES * a : high].astype(jnp.float32)
                if high < LANES * (a + 1):
                    gap = jnp.zeros((many, LANES * (a + 1) - high), jnp.float32)
                    tile = jnp.concatenate([tile, gap], axis=1)
                field[pl.ds(first * FR + a, many, stride=step * FR), :] = tile
        for r in range(rows):
            for c in range(cols):
                v_ref[r * cols + c] = field[cell_rows((r + 1) * width + c + 1), :].astype(jnp.bfloat16)
    else:
        for r in range(rows):
            for c in range(cols):
                field[cell_rows((r + 1) * width + c + 1), :] = own_ref[r * cols + c].astype(jnp.float32)
        for n in range(2):
            for c in range(cols):
                field[cell_rows(out_rows[n] * width + c + 1), :] = row_refs[n][c].astype(jnp.float32)
            for r in range(rows):
                field[cell_rows((r + 1) * width + out_cols[n]), :] = col_refs[n][r].astype(jnp.float32)
    for cell in range((rows + 2) * width):
        totals[cell_rows(cell), :] = zero
    for y in ys:
        y[edge // 8 * 8 :, :] = jnp.zeros((y.shape[0] - edge // 8 * 8, LANES), jnp.float32)

    def gather(g, x):
        for f in range(6):
            at = [cell_rows(table_ref[(g * PACK + s) * 6 + f]) for s in range(PACK)]
            spread = swap_slots([field[at[s], :] for s in range(PACK)])
            for b in range(4):
                x[pl.ds(f * dofs + b, FR, stride=4), :] = spread[b]

    def multiply(g, x, y):
        kind = table_ref[groups * PACK * 6 + g]
        y[0:edge, :] = jnp.dot(
            jac[kind], x[0:edge, :].astype(jnp.bfloat16), preferred_element_type=jnp.float32
        )

    def scatter(g, y):
        for f in range(6):
            back = swap_slots([y[pl.ds(f * dofs + b, FR, stride=4), :] for b in range(4)])
            for s in range(PACK):
                at = cell_rows(table_ref[(g * PACK + s) * 6 + f])
                totals[at, :] = totals[at, :] + back[s]

    def pair(m, carry):
        gather(2 * m, xs[0])
        gather(2 * m + 1, xs[1])
        multiply(2 * m, xs[0], ys[0])
        multiply(2 * m + 1, xs[1], ys[1])
        scatter(2 * m, ys[0])
        scatter(2 * m + 1, ys[1])
        return carry

    done = jnp.int32(0)
    for t in range(kinds):
        fetches[t].wait()
        ready = table_ref[groups * (PACK * 6 + 1) + t]
        upto = (ready + 1) // 2 if t == kinds - 1 else ready // 2
        lax.fori_loop(done, upto, pair, jnp.int32(0))
        done = upto

    for r in range(rows):
        for c in range(cols):
            t_ref[r * cols + c] = totals[cell_rows((r + 1) * width + c + 1), :]
    for n in range(2):
        for c in range(cols):
            to_rows[n][c] = totals[cell_rows(out_rows[n] * width + c + 1), :].astype(jnp.bfloat16)
        for r in range(rows):
            to_cols[n][r] = totals[cell_rows((r + 1) * width + out_cols[n]), :].astype(jnp.bfloat16)


def combine(dims, side_ref, t_ref, rims, hold):
    rows, cols, dofs = dims
    row_edges, col_edges = sides(side_ref, rows, cols)
    for cell in range(rows * cols):
        hold[cell] = t_ref[cell]
    for n in range(2):
        for c in range(cols):
            cell = row_edges[n] * cols + c
            hold[cell] = hold[cell] + rims[n][c].astype(jnp.float32)
        for r in range(rows):
            cell = r * cols + col_edges[n]
            hold[cell] = hold[cell] + rims[2 + n][r].astype(jnp.float32)
    return row_edges, col_edges


def middle_kernel(dims, side_ref, t_ref, a_ref, b_ref, c_ref, d_ref, w_ref, *refs):
    rows, cols, dofs = dims
    hold = refs[-1]
    to_rows, to_cols = refs[0:2], refs[2:4]
    row_edges, col_edges = combine(dims, side_ref, t_ref, (a_ref, b_ref, c_ref, d_ref), hold)
    row = lax.broadcasted_iota(jnp.int32, (FR, LANES), 0)
    slot = lax.broadcasted_iota(jnp.int32, (FR, LANES), 1) // 32
    real = row * 4 + slot < dofs
    for cell in range(rows * cols):
        w_ref[cell] = jnp.where(real, hold[cell], 0.0).astype(jnp.bfloat16)
    for n in range(2):
        for c in range(cols):
            to_rows[n][c] = w_ref[row_edges[n] * cols + c]
        for r in range(rows):
            to_cols[n][r] = w_ref[r * cols + col_edges[n]]


def mail_kernel(dims, v_ref, w_ref, ids_ref, mail_ref):
    rows, cols, dofs = dims
    v = v_ref[...].reshape(rows * cols * FR, LANES)
    w = w_ref[...].reshape(rows * cols * FR, LANES)
    square = lax.dot_general(v, w, (((0,), (0,)), ((), ())), preferred_element_type=jnp.float32)
    side = lax.broadcasted_iota(jnp.int32, (LANES, LANES), 1) // 32
    diagonal = lax.broadcasted_iota(jnp.int32, (LANES, LANES), 0) // 32 == side
    square = jnp.where(diagonal, square, 0.0)
    local = square[0:32] + square[32:64] + square[64:96] + square[96:128]
    local = local + pltpu.roll(local, 64, 1)
    local = (local + pltpu.roll(local, 32, 1)) * (1.0 / math.sqrt(rows * cols * dofs))
    local = jnp.where(diagonal, jnp.concatenate([local] * 4, axis=0), 0.0)
    owners = mail_ref.shape[0]
    ids = ids_ref[...]
    owner = lax.broadcasted_iota(jnp.int32, (owners, LANES), 0)
    vertex = 4 * owner + lax.broadcasted_iota(jnp.int32, (owners, LANES), 1) // 32
    place = (vertex == ids).astype(jnp.bfloat16)
    high = local.astype(jnp.bfloat16)
    low = (local - high.astype(jnp.float32)).astype(jnp.bfloat16)
    values = jnp.dot(place, high, preferred_element_type=jnp.float32) + jnp.dot(
        place, low, preferred_element_type=jnp.float32
    )
    lane = lax.broadcasted_iota(jnp.int32, (owners, LANES), 1)
    halves = jnp.where(lane < 32, ids // 256, ids % 256).astype(jnp.float32)
    mail_ref[...] = jnp.stack([values, halves], axis=1).astype(jnp.bfloat16)


def expand_kernel(mail_ref, out_ref, turned_ref, where_ref, flat_ref, at_ref, hot_ref):
    senders = mail_ref.shape[0]
    vertices = out_ref.shape[2]
    parts = (vertices + LANES - 1) // LANES
    low = lax.broadcasted_iota(jnp.int32, (LANES, senders), 0)
    mail = mail_ref[...].astype(jnp.float32)
    turned_ref[...] = mail[:, 0, :].T
    halves = mail[:, 1, :].T.astype(jnp.int32)
    where_ref[...] = halves[0:32] * 256 + halves[32:64]
    for s in range(32):
        part = slice(s * senders, (s + 1) * senders)
        flat_ref[:, part] = turned_ref[pl.ds(s, 4, stride=32), :]
        ids = where_ref[s : s + 1, :]
        at_ref[:, part] = ids // LANES
        hot_ref[:, part] = (ids % LANES == low).astype(jnp.bfloat16)
    values = flat_ref[...]
    block = at_ref[...]
    left = [jnp.where(block == h, values, 0.0) for h in range(parts)]
    left = jnp.concatenate(left, axis=0).astype(jnp.bfloat16)
    wide = lax.dot_general(
        left, hot_ref[...], (((1,), (1,)), ((), ())), preferred_element_type=jnp.float32
    )
    for h in range(parts):
        total = wide[4 * h : 4 * h + 4]
        high = min(LANES * (h + 1), vertices)
        for j in range(out_ref.shape[0]):
            out_ref[j, :, LANES * h : high] = total[:, 0 : high - LANES * h]


def last_kernel(dims, side_ref, t_ref, a_ref, b_ref, c_ref, d_ref, out_ref, sums, hold):
    rows, cols, dofs = dims
    length = out_ref.shape[2]
    combine(dims, side_ref, t_ref, (a_ref, b_ref, c_ref, d_ref), sums)
    for r in range(rows):
        for c in range(cols):
            hold[pl.ds(r * FR * cols + c, FR, stride=cols), :] = sums[r * cols + c]
    for r in range(rows):
        for a in range(FR):
            high = min(LANES * (a + 1), length)
            start = (r * FR + a) * cols
            tile = hold[start : start + cols, 0 : high - LANES * a]
            out_ref[r, :, LANES * a : high] = tile.astype(jnp.bfloat16)


VM = pl.BlockSpec(memory_space=pltpu.VMEM)
SM = pl.BlockSpec(memory_space=pltpu.SMEM)
HBM = pl.BlockSpec(memory_space=pltpu.HBM)


def struct(shape, dtype=jnp.bfloat16):
    return jax.ShapeDtypeStruct(shape, dtype)


def rim_structs(rows, cols):
    return (
        struct((cols, FR, LANES)),
        struct((cols, FR, LANES)),
        struct((rows, FR, LANES)),
        struct((rows, FR, LANES)),
    )


def apply(flat, dims, side, scalars, own, rims, jacobians):
    rows, cols, dofs = dims
    cells = rows * cols
    slots = scalars[1].shape[0] if flat else 0
    groups = (slots + 3 * 4) // PACK // 2 * 2 if flat else (scalars[0].shape[0] - jacobians.shape[0]) // (PACK * 6 + 1)
    out = (struct((cells, FR, LANES), jnp.float32),) + rim_structs(rows, cols)
    places = (VM,) * 5
    if flat:
        out += (struct((cells, FR, LANES)), struct((groups * (PACK * 6 + 1) + jacobians.shape[0],), jnp.int32))
        places += (VM, SM)
    area = (rows + 2) * (cols + 2) * FR
    flops = 2**34
    moved = jacobians.size * 2 + cells * FR * LANES * 6
    return pl.pallas_call(
        functools.partial(apply_kernel, flat, dims, groups),
        out_shape=out,
        in_specs=[SM] * (1 + len(scalars)) + [VM] * 5 + [HBM],
        out_specs=places,
        scratch_shapes=[
            pltpu.VMEM((area, LANES), jnp.float32),
            pltpu.VMEM((area, LANES), jnp.float32),
            *[pltpu.VMEM((6 * dofs + 10, LANES), jnp.float32)] * 4,
            pltpu.VMEM(jacobians.shape, jnp.bfloat16),
            pltpu.SemaphoreType.DMA((jacobians.shape[0],)),
        ],
        compiler_params=pltpu.CompilerParams(vmem_limit_bytes=VMEM_LIMIT),
        cost_estimate=pl.CostEstimate(flops=flops, bytes_accessed=moved, transcendentals=0),
        name="apply_flat" if flat else "apply_tiles",
    )(side, *scalars, own, *rims, jacobians)


def middle(dims, side, total, rims):
    rows, cols, dofs = dims
    cells = rows * cols
    return pl.pallas_call(
        functools.partial(middle_kernel, dims),
        out_shape=(struct((cells, FR, LANES)),) + rim_structs(rows, cols),
        in_specs=[SM] + [VM] * 5,
        out_specs=(VM,) * 5,
        scratch_shapes=[pltpu.VMEM((cells, FR, LANES), jnp.float32)],
        compiler_params=pltpu.CompilerParams(vmem_limit_bytes=VMEM_LIMIT),
        name="middle",
    )(side, total, *rims)


def make_mail(dims, tiles, first, ids, owners):
    return pl.pallas_call(
        functools.partial(mail_kernel, dims),
        out_shape=struct((owners, 2, LANES)),
        in_specs=[VM] * 3,
        out_specs=VM,
        compiler_params=pltpu.CompilerParams(vmem_limit_bytes=VMEM_LIMIT),
        cost_estimate=pl.CostEstimate(flops=2**30, bytes_accessed=2**20, transcendentals=0),
        name="mail",
    )(tiles, first, ids)


def expand(mail, narrow, vertex_total):
    owned = vertex_total // mail.shape[0]
    return pl.pallas_call(
        expand_kernel,
        out_shape=struct((narrow, owned, vertex_total), jnp.float32),
        in_specs=[VM],
        out_specs=VM,
        scratch_shapes=[
            pltpu.VMEM((LANES, mail.shape[0]), jnp.float32),
            pltpu.VMEM((32, mail.shape[0]), jnp.int32),
            pltpu.VMEM((owned, 32 * mail.shape[0]), jnp.float32),
            pltpu.VMEM((1, 32 * mail.shape[0]), jnp.int32),
            pltpu.VMEM((LANES, 32 * mail.shape[0]), jnp.bfloat16),
        ],
        compiler_params=pltpu.CompilerParams(vmem_limit_bytes=VMEM_LIMIT),
        cost_estimate=pl.CostEstimate(flops=2**30, bytes_accessed=2**18, transcendentals=0),
        name="expand",
    )(mail)


def last(dims, side, total, rims, length):
    rows, cols, dofs = dims
    cells = rows * cols
    return pl.pallas_call(
        functools.partial(last_kernel, dims),
        out_shape=struct((rows, cols, length)),
        in_specs=[SM] + [VM] * 5,
        out_specs=VM,
        scratch_shapes=[
            pltpu.VMEM((cells, FR, LANES), jnp.float32),
            pltpu.VMEM((cells * FR, LANES), jnp.float32),
        ],
        compiler_params=pltpu.CompilerParams(vmem_limit_bytes=VMEM_LIMIT),
        cost_estimate=pl.CostEstimate(flops=2**34, bytes_accessed=2**20, transcendentals=0),
        name="last",
    )(side, total, *rims)


def exchange(row_second, row_first, col_first, col_second):
    def swap(value, axis, start):
        peers = lax.axis_size(axis)
        pairs = [(i, i + 1) for i in range(start, peers - 1, 2)]
        return lax.ppermute(value, axis, pairs + [(j, i) for i, j in pairs])

    return (
        swap(row_second, "sub", 1),
        swap(row_first, "sub", 0),
        swap(col_first, "slab", 0),
        swap(col_second, "slab", 1),
    )


def body(coarse_basis, jacobians, element_faces, element_type, element_count, vertex_ids):
    rows, cols, length = coarse_basis.shape
    dofs = jacobians.shape[1] // 6
    dims = (rows, cols, dofs)
    owners, narrow = lax.axis_size("sub"), lax.axis_size("slab")
    ids = jnp.tile(vertex_ids, (1, 4))
    odd_row, odd_col = lax.axis_index("sub") & 1, lax.axis_index("slab") & 1
    side = jnp.stack([odd_row, odd_col])

    ends = coarse_basis[0], coarse_basis[rows - 1], coarse_basis[:, 0], coarse_basis[:, cols - 1]
    rims = exchange(
        jnp.where(odd_row == 1, ends[1], ends[0]),
        jnp.where(odd_row == 1, ends[0], ends[1]),
        jnp.where(odd_col == 1, ends[2], ends[3]),
        jnp.where(odd_col == 1, ends[3], ends[2]),
    )
    scalars = (element_faces.T, element_type, element_count)
    total, *sent, tiles, table = apply(True, dims, side, scalars, coarse_basis, rims, jacobians)
    first, *halo = middle(dims, side, total, exchange(*sent))
    rims = exchange(*halo)
    tiles, unused = lax.optimization_barrier((tiles, rims[0]))
    mail = lax.all_to_all(make_mail(dims, tiles, first, ids, owners), "sub", 0, 0)
    total, *sent = apply(False, dims, side, (table,), first, rims, jacobians)
    rims = exchange(*sent)
    mail, unused = lax.optimization_barrier((mail, rims[0]))
    parts = lax.all_to_all(expand(mail, narrow, rows * owners), "slab", 0, 0)
    second_image = last(dims, side, total, rims, length)
    return second_image, parts.sum(0)


def solution(mesh):
    return jax.shard_map(
        body,
        mesh=mesh,
        in_specs=(
            P("sub", "slab", None),
            P(),
            P(("sub", "slab"), None),
            P(("sub", "slab")),
            P(("sub", "slab")),
            P(("sub", "slab"), None),
        ),
        out_specs=(P("sub", "slab", None), P("sub", None)),
        check_vma=False,
    )
```

```python
import functools
import math

import jax
import jax.numpy as jnp
from jax import lax
from jax.experimental import pallas as pl
from jax.experimental.pallas import tpu as pltpu
from jax.sharding import PartitionSpec as P

FR = 32
LANES = 128
PACK = 4
VMEM_LIMIT = 20 * 1024 * 1024
WIDE_LIMIT = 50 * 1024 * 1024


def swap_slots(values):
    slot = lax.broadcasted_iota(jnp.int32, values[0].shape, 1) // 32
    upper = slot >= 2
    odd = slot % 2 == 1
    a, b, c, d = values
    a, c = jnp.where(upper, pltpu.roll(c, 64, 1), a), jnp.where(upper, c, pltpu.roll(a, 64, 1))
    b, d = jnp.where(upper, pltpu.roll(d, 64, 1), b), jnp.where(upper, d, pltpu.roll(b, 64, 1))
    a, b = jnp.where(odd, pltpu.roll(b, 32, 1), a), jnp.where(odd, b, pltpu.roll(a, 96, 1))
    c, d = jnp.where(odd, pltpu.roll(d, 32, 1), c), jnp.where(odd, d, pltpu.roll(c, 96, 1))
    return [a, b, c, d]


def make_plan(slots, groups, faces_ref, type_ref, count_ref, table_ref):
    kind_at = groups * PACK * 6
    for i in range(kind_at):
        table_ref[i] = 0
    count = count_ref[0]
    kinds = 4

    def tally(slot, sizes):
        live = slot < count
        return tuple(
            size + (live & (type_ref[slot] == kind)).astype(jnp.int32)
            for kind, size in enumerate(sizes)
        )

    sizes = lax.fori_loop(0, slots, tally, (jnp.int32(0),) * kinds)
    firsts, place = [], jnp.int32(0)
    for kind, size in enumerate(sizes):
        firsts.append(place)
        place = place + (size + PACK - 1) // PACK * PACK
        table_ref[kind_at + groups + kind] = place // PACK

    def put(slot, nexts):
        kind = type_ref[slot]
        position = nexts[kinds - 1]
        for other in range(kinds - 1):
            position = jnp.where(kind == other, nexts[other], position)
        table_ref[kind_at + position // PACK] = kind
        for f in range(6):
            table_ref[position * 6 + f] = faces_ref[f, slot]
        return tuple(at + (kind == other).astype(jnp.int32) for other, at in enumerate(nexts))

    lax.fori_loop(0, count, put, tuple(firsts))


def sides(side_ref, rows, cols):
    odd_row, odd_col = side_ref[0] == 1, side_ref[1] == 1
    first_row = jnp.where(odd_row, 0, rows - 1)
    first_col = jnp.where(odd_col, 0, cols - 1)
    return (rows - 1 - first_row, first_row), (first_col, cols - 1 - first_col)


def beyond(edge, length):
    return jnp.where(edge == 0, 0, length + 1)


def apply_kernel(flat, dims, groups, *refs):
    rows, cols, dofs = dims
    edge = 6 * dofs
    width = cols + 2
    if flat:
        side_ref, faces_ref, type_ref, count_ref, own_ref, *refs = refs
    else:
        side_ref, table_ref, own_ref, *refs = refs
    row_refs, col_refs, jac_hbm, t_ref = refs[0:2], refs[2:4], refs[4], refs[5]
    to_rows, to_cols = refs[6:8], refs[8:10]
    if flat:
        v_ref, table_ref = refs[10:12]
    if flat:
        field, totals, *pairs = refs[-6:]
        jac = jac_hbm
    else:
        field, totals, *pairs, jac, sem = refs[-8:]
    xs, ys = pairs[0:2], pairs[2:4]
    kinds = jac.shape[0]
    fetches = []
    if not flat:
        fetches = [pltpu.make_async_copy(jac_hbm.at[t], jac.at[t], sem.at[t]) for t in range(kinds)]
    for fetch in fetches:
        fetch.start()
    if flat:
        make_plan(type_ref.shape[0], groups, faces_ref, type_ref, count_ref, table_ref)
    row_edges, col_edges = sides(side_ref, rows, cols)
    out_rows = [beyond(r, rows) for r in row_edges]
    out_cols = [beyond(c, cols) for c in col_edges]

    def cell_rows(cell):
        if isinstance(cell, int):
            return slice(cell * FR, (cell + 1) * FR)
        return pl.ds(pl.multiple_of(cell * FR, FR), FR)

    zero = jnp.zeros((FR, LANES), jnp.float32)
    field[0:FR, :] = zero
    if flat:
        sources = [(own_ref.at[r], (r + 1) * width + 1, 1, cols) for r in range(rows)]
        sources += [(row_refs[n], out_rows[n] * width + 1, 1, cols) for n in range(2)]
        sources += [(col_refs[n], width + out_cols[n], width, rows) for n in range(2)]
        for ref, first, step, many in sources:
            length = ref.shape[1]
            for a in range(FR):
                high = min(LANES * (a + 1), length)
                tile = ref[:, LANES * a : high].astype(jnp.float32)
                if high < LANES * (a + 1):
                    gap = jnp.zeros((many, LANES * (a + 1) - high), jnp.float32)
                    tile = jnp.concatenate([tile, gap], axis=1)
                field[pl.ds(first * FR + a, many, stride=step * FR), :] = tile
        for r in range(rows):
            for c in range(cols):
                v_ref[r * cols + c] = field[cell_rows((r + 1) * width + c + 1), :].astype(jnp.bfloat16)
    else:
        for r in range(rows):
            for c in range(cols):
                field[cell_rows((r + 1) * width + c + 1), :] = own_ref[r * cols + c].astype(jnp.float32)
        for n in range(2):
            for c in range(cols):
                field[cell_rows(out_rows[n] * width + c + 1), :] = row_refs[n][c].astype(jnp.float32)
            for r in range(rows):
                field[cell_rows((r + 1) * width + out_cols[n]), :] = col_refs[n][r].astype(jnp.float32)
    for cell in range((rows + 2) * width):
        totals[cell_rows(cell), :] = zero
    for y in ys:
        y[edge // 8 * 8 :, :] = jnp.zeros((y.shape[0] - edge // 8 * 8, LANES), jnp.float32)

    def gather(g, x):
        for f in range(6):
            at = [cell_rows(table_ref[(g * PACK + s) * 6 + f]) for s in range(PACK)]
            spread = swap_slots([field[at[s], :] for s in range(PACK)])
            for b in range(4):
                x[pl.ds(f * dofs + b, FR, stride=4), :] = spread[b]

    def multiply(g, x, y):
        kind = table_ref[groups * PACK * 6 + g]
        y[0:edge, :] = jnp.dot(
            jac[kind], x[0:edge, :].astype(jnp.bfloat16), preferred_element_type=jnp.float32
        )

    def scatter(g, y):
        for f in range(6):
            back = swap_slots([y[pl.ds(f * dofs + b, FR, stride=4), :] for b in range(4)])
            for s in range(PACK):
                at = cell_rows(table_ref[(g * PACK + s) * 6 + f])
                totals[at, :] = totals[at, :] + back[s]

    def pair(m, carry):
        gather(2 * m, xs[0])
        gather(2 * m + 1, xs[1])
        multiply(2 * m, xs[0], ys[0])
        multiply(2 * m + 1, xs[1], ys[1])
        scatter(2 * m, ys[0])
        scatter(2 * m + 1, ys[1])
        return carry

    done = jnp.int32(0)
    for t in range(kinds - 1 if flat else 0, kinds):
        if not flat:
            fetches[t].wait()
        ready = table_ref[groups * (PACK * 6 + 1) + t]
        upto = (ready + 1) // 2 if t == kinds - 1 else ready // 2
        lax.fori_loop(done, upto, pair, jnp.int32(0))
        done = upto

    for r in range(rows):
        for c in range(cols):
            t_ref[r * cols + c] = totals[cell_rows((r + 1) * width + c + 1), :]
    for n in range(2):
        for c in range(cols):
            to_rows[n][c] = totals[cell_rows(out_rows[n] * width + c + 1), :].astype(jnp.bfloat16)
        for r in range(rows):
            to_cols[n][r] = totals[cell_rows((r + 1) * width + out_cols[n]), :].astype(jnp.bfloat16)


def combine(dims, side_ref, t_ref, rims, hold):
    rows, cols, dofs = dims
    row_edges, col_edges = sides(side_ref, rows, cols)
    for cell in range(rows * cols):
        hold[cell] = t_ref[cell]
    for n in range(2):
        for c in range(cols):
            cell = row_edges[n] * cols + c
            hold[cell] = hold[cell] + rims[n][c].astype(jnp.float32)
        for r in range(rows):
            cell = r * cols + col_edges[n]
            hold[cell] = hold[cell] + rims[2 + n][r].astype(jnp.float32)
    return row_edges, col_edges


def middle_kernel(dims, side_ref, t_ref, a_ref, b_ref, c_ref, d_ref, w_ref, *refs):
    rows, cols, dofs = dims
    hold = refs[-1]
    to_rows, to_cols = refs[0:2], refs[2:4]
    row_edges, col_edges = combine(dims, side_ref, t_ref, (a_ref, b_ref, c_ref, d_ref), hold)
    row = lax.broadcasted_iota(jnp.int32, (FR, LANES), 0)
    slot = lax.broadcasted_iota(jnp.int32, (FR, LANES), 1) // 32
    real = row * 4 + slot < dofs
    for cell in range(rows * cols):
        w_ref[cell] = jnp.where(real, hold[cell], 0.0).astype(jnp.bfloat16)
    for n in range(2):
        for c in range(cols):
            to_rows[n][c] = w_ref[row_edges[n] * cols + c]
        for r in range(rows):
            to_cols[n][r] = w_ref[r * cols + col_edges[n]]


def mail_kernel(dims, v_ref, w_ref, ids_ref, mail_ref):
    rows, cols, dofs = dims
    v = v_ref[...].reshape(rows * cols * FR, LANES)
    w = w_ref[...].reshape(rows * cols * FR, LANES)
    square = lax.dot_general(v, w, (((0,), (0,)), ((), ())), preferred_element_type=jnp.float32)
    side = lax.broadcasted_iota(jnp.int32, (LANES, LANES), 1) // 32
    diagonal = lax.broadcasted_iota(jnp.int32, (LANES, LANES), 0) // 32 == side
    square = jnp.where(diagonal, square, 0.0)
    local = square[0:32] + square[32:64] + square[64:96] + square[96:128]
    local = local + pltpu.roll(local, 64, 1)
    local = (local + pltpu.roll(local, 32, 1)) * (1.0 / math.sqrt(rows * cols * dofs))
    local = jnp.where(diagonal, jnp.concatenate([local] * 4, axis=0), 0.0)
    owners = mail_ref.shape[0]
    ids = ids_ref[...]
    owner = lax.broadcasted_iota(jnp.int32, (owners, LANES), 0)
    vertex = 4 * owner + lax.broadcasted_iota(jnp.int32, (owners, LANES), 1) // 32
    place = (vertex == ids).astype(jnp.bfloat16)
    high = local.astype(jnp.bfloat16)
    low = (local - high.astype(jnp.float32)).astype(jnp.bfloat16)
    values = jnp.dot(place, high, preferred_element_type=jnp.float32) + jnp.dot(
        place, low, preferred_element_type=jnp.float32
    )
    lane = lax.broadcasted_iota(jnp.int32, (owners, LANES), 1)
    halves = jnp.where(lane < 32, ids // 256, ids % 256).astype(jnp.float32)
    mail_ref[...] = jnp.stack([values, halves], axis=1).astype(jnp.bfloat16)


def expand_kernel(mail_ref, out_ref, turned_ref, where_ref, flat_ref, at_ref, hot_ref):
    senders = mail_ref.shape[0]
    vertices = out_ref.shape[2]
    parts = (vertices + LANES - 1) // LANES
    low = lax.broadcasted_iota(jnp.int32, (LANES, senders), 0)
    mail = mail_ref[...].astype(jnp.float32)
    turned_ref[...] = mail[:, 0, :].T
    halves = mail[:, 1, :].T.astype(jnp.int32)
    where_ref[...] = halves[0:32] * 256 + halves[32:64]
    for s in range(32):
        part = slice(s * senders, (s + 1) * senders)
        flat_ref[:, part] = turned_ref[pl.ds(s, 4, stride=32), :]
        ids = where_ref[s : s + 1, :]
        at_ref[:, part] = ids // LANES
        hot_ref[:, part] = (ids % LANES == low).astype(jnp.bfloat16)
    values = flat_ref[...]
    block = at_ref[...]
    left = [jnp.where(block == h, values, 0.0) for h in range(parts)]
    left = jnp.concatenate(left, axis=0).astype(jnp.bfloat16)
    wide = lax.dot_general(
        left, hot_ref[...], (((1,), (1,)), ((), ())), preferred_element_type=jnp.float32
    )
    for h in range(parts):
        total = wide[4 * h : 4 * h + 4]
        high = min(LANES * (h + 1), vertices)
        for j in range(out_ref.shape[0]):
            out_ref[j, :, LANES * h : high] = total[:, 0 : high - LANES * h]


def last_kernel(dims, side_ref, t_ref, a_ref, b_ref, c_ref, d_ref, out_ref, sums, hold):
    rows, cols, dofs = dims
    length = out_ref.shape[2]
    combine(dims, side_ref, t_ref, (a_ref, b_ref, c_ref, d_ref), sums)
    for r in range(rows):
        for c in range(cols):
            hold[pl.ds(r * FR * cols + c, FR, stride=cols), :] = sums[r * cols + c]
    for r in range(rows):
        for a in range(FR):
            high = min(LANES * (a + 1), length)
            start = (r * FR + a) * cols
            tile = hold[start : start + cols, 0 : high - LANES * a]
            out_ref[r, :, LANES * a : high] = tile.astype(jnp.bfloat16)


VM = pl.BlockSpec(memory_space=pltpu.VMEM)
SM = pl.BlockSpec(memory_space=pltpu.SMEM)
HBM = pl.BlockSpec(memory_space=pltpu.HBM)


def struct(shape, dtype=jnp.bfloat16):
    return jax.ShapeDtypeStruct(shape, dtype)


def rim_structs(rows, cols):
    return (
        struct((cols, FR, LANES)),
        struct((cols, FR, LANES)),
        struct((rows, FR, LANES)),
        struct((rows, FR, LANES)),
    )


def apply(flat, dims, side, scalars, own, rims, jacobians):
    rows, cols, dofs = dims
    cells = rows * cols
    slots = scalars[1].shape[0] if flat else 0
    groups = (slots + 3 * 4) // PACK // 2 * 2 if flat else (scalars[0].shape[0] - jacobians.shape[0]) // (PACK * 6 + 1)
    out = (struct((cells, FR, LANES), jnp.float32),) + rim_structs(rows, cols)
    places = (VM,) * 5
    if flat:
        out += (struct((cells, FR, LANES)), struct((groups * (PACK * 6 + 1) + jacobians.shape[0],), jnp.int32))
        places += (VM, SM)
    area = (rows + 2) * (cols + 2) * FR
    held = [pltpu.VMEM(jacobians.shape, jnp.bfloat16), pltpu.SemaphoreType.DMA((jacobians.shape[0],))]
    flops = 2**34
    moved = jacobians.size * 2 + cells * FR * LANES * 6
    return pl.pallas_call(
        functools.partial(apply_kernel, flat, dims, groups),
        out_shape=out,
        in_specs=[SM] * (1 + len(scalars)) + [VM] * 5 + [VM if flat else HBM],
        out_specs=places,
        scratch_shapes=[
            pltpu.VMEM((area, LANES), jnp.float32),
            pltpu.VMEM((area, LANES), jnp.float32),
            *[pltpu.VMEM((6 * dofs + 10, LANES), jnp.float32)] * 4,
            *([] if flat else held),
        ],
        compiler_params=pltpu.CompilerParams(vmem_limit_bytes=VMEM_LIMIT if flat else WIDE_LIMIT),
        cost_estimate=pl.CostEstimate(flops=flops, bytes_accessed=moved, transcendentals=0),
        name="apply_flat" if flat else "apply_tiles",
    )(side, *scalars, own, *rims, jacobians)


def middle(dims, side, total, rims):
    rows, cols, dofs = dims
    cells = rows * cols
    return pl.pallas_call(
        functools.partial(middle_kernel, dims),
        out_shape=(struct((cells, FR, LANES)),) + rim_structs(rows, cols),
        in_specs=[SM] + [VM] * 5,
        out_specs=(VM,) * 5,
        scratch_shapes=[pltpu.VMEM((cells, FR, LANES), jnp.float32)],
        compiler_params=pltpu.CompilerParams(vmem_limit_bytes=VMEM_LIMIT),
        name="middle",
    )(side, total, *rims)


def make_mail(dims, tiles, first, ids, owners):
    return pl.pallas_call(
        functools.partial(mail_kernel, dims),
        out_shape=struct((owners, 2, LANES)),
        in_specs=[VM] * 3,
        out_specs=VM,
        compiler_params=pltpu.CompilerParams(vmem_limit_bytes=VMEM_LIMIT),
        cost_estimate=pl.CostEstimate(flops=2**30, bytes_accessed=2**20, transcendentals=0),
        name="mail",
    )(tiles, first, ids)


def expand(mail, narrow, vertex_total):
    owned = vertex_total // mail.shape[0]
    return pl.pallas_call(
        expand_kernel,
        out_shape=struct((narrow, owned, vertex_total), jnp.float32),
        in_specs=[VM],
        out_specs=VM,
        scratch_shapes=[
            pltpu.VMEM((LANES, mail.shape[0]), jnp.float32),
            pltpu.VMEM((32, mail.shape[0]), jnp.int32),
            pltpu.VMEM((owned, 32 * mail.shape[0]), jnp.float32),
            pltpu.VMEM((1, 32 * mail.shape[0]), jnp.int32),
            pltpu.VMEM((LANES, 32 * mail.shape[0]), jnp.bfloat16),
        ],
        compiler_params=pltpu.CompilerParams(vmem_limit_bytes=VMEM_LIMIT),
        cost_estimate=pl.CostEstimate(flops=2**30, bytes_accessed=2**18, transcendentals=0),
        name="expand",
    )(mail)


def last(dims, side, total, rims, length):
    rows, cols, dofs = dims
    cells = rows * cols
    return pl.pallas_call(
        functools.partial(last_kernel, dims),
        out_shape=struct((rows, cols, length)),
        in_specs=[SM] + [VM] * 5,
        out_specs=VM,
        scratch_shapes=[
            pltpu.VMEM((cells, FR, LANES), jnp.float32),
            pltpu.VMEM((cells * FR, LANES), jnp.float32),
        ],
        compiler_params=pltpu.CompilerParams(vmem_limit_bytes=VMEM_LIMIT),
        cost_estimate=pl.CostEstimate(flops=2**34, bytes_accessed=2**20, transcendentals=0),
        name="last",
    )(side, total, *rims)


def exchange(row_second, row_first, col_first, col_second):
    def swap(value, axis, start):
        peers = lax.axis_size(axis)
        pairs = [(i, i + 1) for i in range(start, peers - 1, 2)]
        return lax.ppermute(value, axis, pairs + [(j, i) for i, j in pairs])

    return (
        swap(row_second, "sub", 1),
        swap(row_first, "sub", 0),
        swap(col_first, "slab", 0),
        swap(col_second, "slab", 1),
    )


def body(coarse_basis, jacobians, element_faces, element_type, element_count, vertex_ids):
    rows, cols, length = coarse_basis.shape
    dofs = jacobians.shape[1] // 6
    dims = (rows, cols, dofs)
    owners, narrow = lax.axis_size("sub"), lax.axis_size("slab")
    ids = jnp.tile(vertex_ids, (1, 4))
    odd_row, odd_col = lax.axis_index("sub") & 1, lax.axis_index("slab") & 1
    side = jnp.stack([odd_row, odd_col])

    ends = coarse_basis[0], coarse_basis[rows - 1], coarse_basis[:, 0], coarse_basis[:, cols - 1]
    rims = exchange(
        jnp.where(odd_row == 1, ends[1], ends[0]),
        jnp.where(odd_row == 1, ends[0], ends[1]),
        jnp.where(odd_col == 1, ends[2], ends[3]),
        jnp.where(odd_col == 1, ends[3], ends[2]),
    )
    scalars = (element_faces.T, element_type, element_count)
    total, *sent, tiles, table = apply(True, dims, side, scalars, coarse_basis, rims, jacobians)
    first, *halo = middle(dims, side, total, exchange(*sent))
    rims = exchange(*halo)
    tiles, unused = lax.optimization_barrier((tiles, rims[0]))
    mail = lax.all_to_all(make_mail(dims, tiles, first, ids, owners), "sub", 0, 0)
    total, *sent = apply(False, dims, side, (table,), first, rims, jacobians)
    rims = exchange(*sent)
    mail, unused = lax.optimization_barrier((mail, rims[0]))
    parts = lax.all_to_all(expand(mail, narrow, rows * owners), "slab", 0, 0)
    second_image = last(dims, side, total, rims, length)
    return second_image, parts.sum(0)


def solution(mesh):
    return jax.shard_map(
        body,
        mesh=mesh,
        in_specs=(
            P("sub", "slab", None),
            P(),
            P(("sub", "slab"), None),
            P(("sub", "slab")),
            P(("sub", "slab")),
            P(("sub", "slab"), None),
        ),
        out_specs=(P("sub", "slab", None), P("sub", None)),
        check_vma=False,
    )
```
